32 devices in a mesh: groups: 2 (over y), space: 4 (over x, core), frame: 4 (over z).
Axes of the slice: x: 2, y: 2, z: 4, core: 2. Of those that a mesh axis runs over, the one named last changes fastest.
Arguments:
- clip: bfloat16 [8, 24, 32, 512], P(('groups', 'frame'), 'space'), parts along dimension 0, may hold values from -6 to 6
- cotangent: bfloat16 [8, 24, 32, 512], P(('groups', 'frame'), 'space'), parts along dimension 0, may hold values from -6 to 6
- tile_rows: int32 [8], P('groups'), parts along dimension 0, may hold values from 1 to 6, 12 in all
- frame_start: int32 [8, 32], P('groups'), parts along dimension 0, may hold values from 0 to 3, as said below
- norm_gain: float32 [512], replicated, may hold values from 0.1 to 1.9
- w_spatial: bfloat16 [9, 512, 512], P(None, 'space'), may hold values from -0.09375 to 0.09375
- w_temporal: bfloat16 [3, 512, 512], P(None, 'space'), may hold values from -0.15625 to 0.15625
- w_attn: bfloat16 [4, 512, 512], P(None, 'space'), may hold values from -0.25 to 0.25
Outputs:
- block_output: bfloat16 [8, 24, 32, 512], P(('groups', 'frame'), 'space'), parts along dimension 0
- clip_grad: bfloat16 [8, 24, 32, 512], P(('groups', 'frame'), 'space'), parts along dimension 0
The draws below stay inside these ranges and needn't reach their ends.
There are 2 independent parts, one for each index of `groups`. The reference program is written for one: setup_inputs(seed, part) draws one part's arguments, and reference() takes and returns one part's arrays. A program takes and returns all parts, laid end to end along the dimension named above; an argument that names none is the same for every part. Nothing has to cross between parts.
Inputs may be any that keep to these rules, and one draw needn't show every extreme that they name: tile_rows[t] counts the frame rows of tile t, tiles in order down the frame; they sum to 12 and the largest is 6. frame_start[f,j] <= f for every frame f and column j; column 0 of the last frame starts at 3.
All inputs are finite; a program needn't handle non-finite values.
Results may differ from the reference program's by a relative error of at most 0.014.
Values may be sent and summed in bfloat16 or wider, within the bound.
A program may use at most 64 MiB of HBM per device.

```python
import math
import jax
import jax.numpy as jnp
import numpy as np
from jax import lax

C = 512
WIN = 32
R_MAX = 6
FRAME_ROWS = 12
SLOTS = 24
FRAMES = 4
N_SPACE = 4


def draw_frame_start(key, part):
    limits = jnp.broadcast_to((jnp.arange(FRAMES, dtype=jnp.int32) + 1)[:, None], (FRAMES, WIN))
    drawn = jax.random.randint(key, (FRAMES, WIN), 0, limits).astype(jnp.int32)
    rows = jnp.arange(FRAMES, dtype=jnp.int32)[:, None]
    cols = jnp.arange(WIN, dtype=jnp.int32)[None, :]
    return jnp.where((rows == FRAMES - 1) & (cols == 0), FRAMES - 1, drawn).astype(jnp.int32)


def steps_of(key, extent, pieces, low, high):
    loudness = 1.0
    for position, parts in pieces:
        heights = jax.random.uniform(jax.random.fold_in(jax.random.fold_in(key, 6), position), (parts,), jnp.float32, low / len(pieces), high / len(pieces))
        loudness = loudness * jnp.repeat(jnp.exp(heights), extent[position] // parts).reshape((-1,) + (1,) * (len(extent) - 1 - position))
    return loudness


def split_up(count, total, limit, slope):
    weights = [(1 << 20) // math.isqrt(standing ** slope) + 1 for standing in range(2, count + 1)]
    spare, holding = total - limit - (count - 1), [1] * (count - 1)
    while spare > 0:
        candidates = [i for i in range(count - 1) if holding[i] < limit]
        pool, budget = sum([weights[i] for i in candidates]), spare
        for i in candidates:
            more = min(limit - holding[i], max(1, budget * weights[i] // pool), spare)
            holding[i] = holding[i] + more
            spare = spare - more
    return np.array([limit] + holding)


def uneven(stream_key, number_of, total, reach, slope):
    if number_of == 2:
        one = jax.random.randint(stream_key, (), max(1, total - reach), min(reach, total - 1) + 1)
        return jnp.stack([one, total - one])
    lengths = jnp.asarray(split_up(number_of, total, reach, slope), jnp.int32)
    couples = (number_of - 1) // 2
    donor, taker = lengths[1:1 + 2 * couples:2], lengths[2:2 + 2 * couples:2]
    room = jnp.minimum(donor - 1, reach - taker)
    shifted = jax.random.randint(jax.random.fold_in(stream_key, 1), (couples,), 0, 1 << 20) % (room + 1)
    lengths = lengths.at[1:1 + 2 * couples:2].set(donor - shifted).at[2:2 + 2 * couples:2].set(taker + shifted)
    return lengths[jax.random.permutation(jax.random.fold_in(stream_key, 2), number_of)]


def scatter_about(stream_key, shape, spread, bound, shards=(), kind=jnp.bfloat16):
    values = spread * jax.random.normal(stream_key, shape, jnp.float32)
    if shards:
        values = values * steps_of(stream_key, shape, shards, -0.22, 0.18)
    return jnp.clip(values, -bound, bound).astype(kind)


def setup_inputs(seed: int = 0, part: int = 0) -> dict:
    arg_keys = jax.random.split(jax.random.key(seed), 9)
    part_splits = jax.random.split(jax.random.fold_in(arg_keys[8], part), 9)
    clip = scatter_about(part_splits[0], (FRAMES, SLOTS, WIN, C), 1.0, 6.0, ((0, 4), (1, 4)))
    cotangent = scatter_about(part_splits[1], (FRAMES, SLOTS, WIN, C), 1.0, 6.0, ((0, 4), (1, 4)))
    tile_rows = uneven(part_splits[2], N_SPACE, FRAME_ROWS, R_MAX, 2).astype(jnp.int32)
    frame_start = draw_frame_start(jax.random.fold_in(jax.random.fold_in(arg_keys[8], part), 71), part)
    norm_gain = jnp.clip(1.0 + 0.18 * jax.random.normal(arg_keys[4], (C,), jnp.float32), 0.1, 1.9)
    w_spatial = scatter_about(arg_keys[5], (9, C, C), (9 * C) ** -0.5, 0.09375, ((1, 4),))
    w_temporal = scatter_about(arg_keys[6], (3, C, C), (3 * C) ** -0.5, 0.15625, ((1, 4),))
    w_attn = scatter_about(arg_keys[7], (4, C, C), C ** -0.5, 0.25, ((1, 4),))
    return {"clip": clip, "cotangent": cotangent, "tile_rows": tile_rows, "frame_start": frame_start, "norm_gain": norm_gain, "w_spatial": w_spatial, "w_temporal": w_temporal, "w_attn": w_attn}


NORM_EPSILON = 1e-06

def apply_matrix(values, matrix):
    return jnp.einsum('fhwd,de->fhwe', values.astype(jnp.float32), matrix.astype(jnp.float32))

def apply_back(values, matrix):
    return jnp.einsum('fhwe,de->fhwd', values.astype(jnp.float32), matrix.astype(jnp.float32))

def conv_frames(source, kernel, flipped):
    height = source.shape[1]
    breadth = source.shape[2]
    padded = jnp.pad(source, ((0, 0), (1, 1), (1, 1), (0, 0)))
    summed = jnp.zeros(source.shape, jnp.float32)
    for tap_row in range(3):
        for tap_col in range(3):
            patches = padded[:, tap_row:tap_row + height, tap_col:tap_col + breadth]
            if flipped:
                summed = summed + apply_back(patches, kernel[(2 - tap_row) * 3 + 2 - tap_col])
            else:
                summed = summed + apply_matrix(patches, kernel[tap_row * 3 + tap_col])
    return summed

def reference(clip, cotangent, tile_rows, frame_start, norm_gain, w_spatial, w_temporal, w_attn):
    frames = clip.shape[0]
    slots = clip.shape[1]
    channels = clip.shape[3]
    tile_height = slots // N_SPACE
    score_scale = channels ** (-0.5)
    bounds = (jnp.cumsum(tile_rows) - tile_rows).astype(jnp.int32)
    global_rows = jnp.arange(FRAME_ROWS, dtype=jnp.int32)
    tile_ids = jnp.arange(N_SPACE, dtype=jnp.int32)
    owner = (lax.optimization_barrier(jnp.sum((bounds[None, :] <= global_rows[:, None]).astype(jnp.int32), 1)) - 1).astype(jnp.int32)
    owner_start = lax.optimization_barrier(jnp.sum(jnp.where(tile_ids[None, :] == owner[:, None], bounds[None, :], 0), 1)).astype(jnp.int32)
    slot_of_row = (owner * tile_height + global_rows - owner_start).astype(jnp.int32)
    slot_ids = jnp.arange(slots, dtype=jnp.int32)
    slot_tile = (slot_ids // tile_height).astype(jnp.int32)
    slot_offset = (slot_ids - slot_tile * tile_height).astype(jnp.int32)
    live = slot_offset < tile_rows[slot_tile]
    row_of_slot = jnp.minimum(bounds[slot_tile] + slot_offset, FRAME_ROWS - 1).astype(jnp.int32)
    inputs = clip[:, slot_of_row].astype(jnp.float32)
    grad_out = cotangent[:, slot_of_row]
    inverse = lax.rsqrt(lax.optimization_barrier(jnp.mean(inputs * inputs, -1, keepdims=True)) + NORM_EPSILON)
    normed = inputs * inverse
    hidden = (normed * norm_gain).astype(jnp.bfloat16)
    preact = conv_frames(hidden, w_spatial, False)
    activated = jax.nn.silu(preact).astype(jnp.bfloat16)
    padded_act = jnp.pad(activated, ((2, 0), (0, 0), (0, 0), (0, 0)))
    mixed = apply_matrix(padded_act[2:2 + frames], w_temporal[0]) + apply_matrix(padded_act[1:1 + frames], w_temporal[1]) + apply_matrix(padded_act[0:frames], w_temporal[2])
    residual = (inputs + mixed).astype(jnp.bfloat16)
    queries = apply_matrix(residual, w_attn[0]).astype(jnp.bfloat16)
    keys_all = apply_matrix(residual, w_attn[1]).astype(jnp.bfloat16)
    values_all = apply_matrix(residual, w_attn[2]).astype(jnp.bfloat16)
    frame_ids = jnp.arange(frames, dtype=jnp.int32)
    allowed = (frame_ids[None, :, None] >= frame_start[:, None, :]) & (frame_ids[None, :, None] <= frame_ids[:, None, None])
    scores = jnp.einsum('fhwc,ghwc->fghw', queries.astype(jnp.float32), keys_all.astype(jnp.float32)) * score_scale
    scores = jnp.where(allowed[:, :, None, :], scores, -jnp.inf)
    probs = jax.nn.softmax(scores, axis=1)
    probs_low = probs.astype(jnp.bfloat16)
    attended = jnp.einsum('fghw,ghwc->fhwc', probs_low.astype(jnp.float32), values_all.astype(jnp.float32)).astype(jnp.bfloat16)
    block_out = (residual.astype(jnp.float32) + apply_matrix(attended, w_attn[3])).astype(jnp.bfloat16)
    grad_attended = apply_back(grad_out, w_attn[3]).astype(jnp.bfloat16)
    grad_probs = jnp.einsum('fhwc,ghwc->fghw', grad_attended.astype(jnp.float32), values_all.astype(jnp.float32))
    grad_scores = probs * (grad_probs - lax.optimization_barrier(jnp.sum(probs * grad_probs, 1, keepdims=True)))
    grad_scores_low = grad_scores.astype(jnp.bfloat16)
    grad_queries = (jnp.einsum('fghw,ghwc->fhwc', grad_scores_low.astype(jnp.float32), keys_all.astype(jnp.float32)) * score_scale).astype(jnp.bfloat16)

    def add_terms(carry, query_frame):
        score_row, weight_row, query_row, grad_row = query_frame
        grad_keys = score_row.astype(jnp.float32)[..., None] * query_row.astype(jnp.float32)[None] * score_scale
        grad_values = weight_row.astype(jnp.float32)[..., None] * grad_row.astype(jnp.float32)[None]
        rounded = jnp.concatenate([grad_keys, grad_values], -1).astype(jnp.bfloat16)
        rounded = lax.optimization_barrier(rounded)
        return (carry + rounded.astype(jnp.float32), None)
    start_carry = jnp.zeros((frames, FRAME_ROWS, clip.shape[2], 2 * channels), jnp.float32)
    key_sums, _ = lax.scan(add_terms, start_carry, (grad_scores_low, probs_low, queries, grad_attended))
    grad_keys_low = key_sums[..., :channels].astype(jnp.bfloat16)
    grad_values_low = key_sums[..., channels:].astype(jnp.bfloat16)
    grad_resid = grad_out.astype(jnp.float32) + apply_back(grad_queries, w_attn[0]) + apply_back(grad_keys_low, w_attn[1]) + apply_back(grad_values_low, w_attn[2])
    grad_low = grad_resid.astype(jnp.bfloat16)
    padded_grad = jnp.pad(grad_low, ((0, 2), (0, 0), (0, 0), (0, 0)))
    grad_act = apply_back(padded_grad[0:frames], w_temporal[0]) + apply_back(padded_grad[1:1 + frames], w_temporal[1]) + apply_back(padded_grad[2:2 + frames], w_temporal[2])
    sigmoid_pre = jax.nn.sigmoid(preact)
    grad_pre = (grad_act * sigmoid_pre * (1.0 + preact * (1.0 - sigmoid_pre))).astype(jnp.bfloat16)
    grad_hidden = conv_frames(grad_pre, w_spatial, True)
    grad_normed = grad_hidden * norm_gain
    grad_inputs = inverse * (grad_normed - normed * lax.optimization_barrier(jnp.mean(grad_normed * normed, -1, keepdims=True)))
    clip_grad = (grad_resid + grad_inputs).astype(jnp.bfloat16)
    live_mask = live[None, :, None, None]
    out_slots = jnp.where(live_mask, block_out[:, row_of_slot], jnp.zeros((), jnp.bfloat16)).astype(jnp.bfloat16)
    grad_slots = jnp.where(live_mask, clip_grad[:, row_of_slot], jnp.zeros((), jnp.bfloat16)).astype(jnp.bfloat16)
    return (out_slots, grad_slots)
```

```python
import functools

import jax
import jax.numpy as jnp
from jax import lax
from jax.experimental import pallas as pl
from jax.experimental.pallas import tpu as pltpu
from jax.sharding import PartitionSpec as P

NORM_EPSILON = 1e-06


def passed_along(value, axis, steps):
    count = lax.axis_size(axis)
    first, last = (max(0, -steps), min(count, count - steps))
    return lax.ppermute(value, axis, [(source, source + steps) for source in range(first, last)])


def tile_rim(edge_row, offset):
    return passed_along(edge_row, "space", offset)


def frame_rim(values, offset):
    return passed_along(values, "frame", offset)


def with_faces(values, row_count):
    height = values.shape[0]
    lowest = lax.dynamic_index_in_dim(values, row_count - 1, 0, keepdims=False)
    upper_face = tile_rim(lowest, 1)
    lower_face = tile_rim(values[0], -1)
    extended = jnp.concatenate([upper_face[None], values, jnp.zeros_like(values[:1])], 0)
    position = lax.broadcasted_iota(jnp.int32, (height + 2, 1, 1), 0)
    extended = jnp.where(position == row_count + 1, lower_face[None], extended)
    return jnp.pad(extended, ((0, 0), (1, 1), (0, 0)))


def spatial_conv(extended, kernel, flipped):
    height = extended.shape[0] - 2
    breadth = extended.shape[1] - 2
    summed = None
    for tap_row in range(3):
        for tap_col in range(3):
            patches = extended[tap_row : tap_row + height, tap_col : tap_col + breadth]
            if flipped:
                product = jnp.einsum(
                    "hwd,ed->hwe",
                    patches,
                    kernel[(2 - tap_row) * 3 + 2 - tap_col],
                    preferred_element_type=jnp.float32,
                )
            else:
                product = jnp.einsum(
                    "hwd,de->hwe",
                    patches,
                    kernel[tap_row * 3 + tap_col],
                    preferred_element_type=jnp.float32,
                )
            summed = product if summed is None else summed + product
    return summed


def project(values, matrix):
    return jnp.einsum("hwd,de->hwe", values, matrix, preferred_element_type=jnp.float32)


def project_back(values, matrix):
    return jnp.einsum("hwe,de->hwd", values, matrix, preferred_element_type=jnp.float32)


def per_device(clip, cotangent, tile_rows, frame_start, norm_gain, w_spatial, w_temporal, w_attn):
    height = clip.shape[1]
    breadth = clip.shape[2]
    channels = clip.shape[3]
    frames = lax.axis_size("frame")
    frame_now = lax.axis_index("frame")
    row_count = tile_rows[lax.axis_index("space")]
    live = (lax.broadcasted_iota(jnp.int32, (height, 1, 1), 0) < row_count).astype(jnp.float32)
    score_scale = channels ** (-0.5)
    kernel, temporal, attention = (
        lax.all_gather(w_spatial, "space", axis=1, tiled=True),
        lax.all_gather(w_temporal, "space", axis=1, tiled=True),
        lax.all_gather(w_attn, "space", axis=1, tiled=True),
    )
    inputs = clip[0].astype(jnp.float32)
    inverse = lax.rsqrt(jnp.mean(inputs * inputs, -1, keepdims=True) + NORM_EPSILON)
    normed = inputs * inverse
    hidden = (normed * norm_gain * live).astype(jnp.bfloat16)
    preact = spatial_conv(with_faces(hidden, row_count), kernel, False) * live
    activated = jax.nn.silu(preact).astype(jnp.bfloat16)
    mixed = (
        project(activated, temporal[0])
        + project(frame_rim(activated, 1), temporal[1])
        + project(frame_rim(activated, 2), temporal[2])
    )
    residual = ((inputs + mixed) * live).astype(jnp.bfloat16)
    queries = project(residual, attention[0]).astype(jnp.bfloat16)
    keys_own = project(residual, attention[1]).astype(jnp.bfloat16)
    values_own = project(residual, attention[2]).astype(jnp.bfloat16)
    upstream = cotangent[0].astype(jnp.float32) * live
    grad_out = upstream.astype(jnp.bfloat16)
    grad_attended = project_back(grad_out, attention[3]).astype(jnp.bfloat16)
    pixels = height * breadth
    share = pixels // frames
    outgoing = jnp.stack(
        [
            queries.reshape(1, pixels, channels),
            keys_own.reshape(1, pixels, channels),
            values_own.reshape(1, pixels, channels),
            grad_attended.reshape(1, pixels, channels),
        ]
    )
    arrived = lax.all_to_all(outgoing, "frame", split_axis=2, concat_axis=1, tiled=True)
    query_all = arrived[0]
    key_all = arrived[1]
    value_all = arrived[2]
    upward_all = arrived[3]
    frame_ids = lax.iota(jnp.int32, frames)
    columns = (frame_now * share + lax.iota(jnp.int32, share)) % breadth
    starts = jnp.take(frame_start, columns, axis=1)
    allowed = (frame_ids[None, :, None] >= starts[:, None, :]) & (
        frame_ids[None, :, None] <= frame_ids[:, None, None]
    )
    scores = (
        jnp.einsum("fpc,gpc->fgp", query_all, key_all, preferred_element_type=jnp.float32)
        * score_scale
    )
    scores = jnp.where(allowed, scores, -jnp.inf)
    probs = jax.nn.softmax(scores, axis=1)
    probs_low = probs.astype(jnp.bfloat16)
    attended_all = jnp.einsum(
        "fgp,gpc->fpc", probs_low, value_all, preferred_element_type=jnp.float32
    ).astype(jnp.bfloat16)
    grad_probs = jnp.einsum(
        "fpc,gpc->fgp", upward_all, value_all, preferred_element_type=jnp.float32
    )
    grad_scores = probs * (grad_probs - jnp.sum(probs * grad_probs, 1, keepdims=True))
    grad_scores_low = grad_scores.astype(jnp.bfloat16)
    grad_query_all = (
        jnp.einsum("fgp,gpc->fpc", grad_scores_low, key_all, preferred_element_type=jnp.float32)
        * score_scale
    ).astype(jnp.bfloat16)
    key_terms = (
        jnp.einsum("fgp,fpc->fgpc", grad_scores_low, query_all, preferred_element_type=jnp.float32)
        * score_scale
    ).astype(jnp.bfloat16)
    grad_key_all = jnp.sum(key_terms.astype(jnp.float32), 0).astype(jnp.bfloat16)
    value_terms = jnp.einsum(
        "fgp,fpc->fgpc", probs_low, upward_all, preferred_element_type=jnp.float32
    ).astype(jnp.bfloat16)
    grad_value_all = jnp.sum(value_terms.astype(jnp.float32), 0).astype(jnp.bfloat16)
    returning = jnp.stack([attended_all, grad_query_all, grad_key_all, grad_value_all])
    came_back = lax.all_to_all(returning, "frame", split_axis=1, concat_axis=2, tiled=True)
    attended = came_back[0, 0].reshape(height, breadth, channels)
    grad_queries = came_back[1, 0].reshape(height, breadth, channels)
    grad_keys_low = came_back[2, 0].reshape(height, breadth, channels)
    grad_values_low = came_back[3, 0].reshape(height, breadth, channels)
    block_output = ((residual.astype(jnp.float32) + project(attended, attention[3])) * live).astype(
        jnp.bfloat16
    )
    grad_resid = (
        upstream
        + project_back(grad_queries, attention[0])
        + project_back(grad_keys_low, attention[1])
        + project_back(grad_values_low, attention[2])
    )
    grad_resid = grad_resid * live
    grad_low = grad_resid.astype(jnp.bfloat16)
    grad_act = (
        project_back(grad_low, temporal[0])
        + project_back(frame_rim(grad_low, -1), temporal[1])
        + project_back(frame_rim(grad_low, -2), temporal[2])
    )
    sigmoid_pre = jax.nn.sigmoid(preact)
    grad_pre = (grad_act * sigmoid_pre * (1.0 + preact * (1.0 - sigmoid_pre)) * live).astype(
        jnp.bfloat16
    )
    grad_hidden = spatial_conv(with_faces(grad_pre, row_count), kernel, True)
    grad_normed = grad_hidden * norm_gain
    grad_inputs = inverse * (
        grad_normed - normed * jnp.mean(grad_normed * normed, -1, keepdims=True)
    )
    clip_grad = ((grad_resid + grad_inputs) * live).astype(jnp.bfloat16)
    return (block_output[None], clip_grad[None])


MESH_ID = pl.DeviceIdType.MESH
LOW = jnp.bfloat16
WIDE = jnp.float32
ROW_PAD = 16
SLOT_PAD = 8


def dot_plain(left, right):
    return jnp.dot(left, right, preferred_element_type=WIDE)


def dot_back(left, right):
    return lax.dot_general(left, right, (((1,), (1,)), ((), ())), preferred_element_type=WIDE)


def strip_kernel(
    n, frames, cs, cf, taps_total,
    pick, place, gain, bias, keep, clip_in, cot_in, ws_in, wt_in, wa_in,
    out_block, out_grad,
    weights, clip_slab, cot_slab, clip_comp, cot_comp, clip_all, cot_all,
    shifted, pre, act_pad, resid, qs, ks, gs, att, gres, glow_pad, ghid,
    block_own, grad_own, block_z, grad_z, block_slab, grad_slab,
    x_s, x_r, c0_s, c0_r, y_s, y_r, c1_s, c1_r, c2_s, c2_r, w_loc,
    p1_s, p1_r, p1_l, p2_s, p2_r, p2_l, oz_s, oz_r, oz_l, ox_s, ox_r, ox_l,
):
    space = lax.axis_index("space")
    frame = lax.axis_index("frame")
    group = lax.axis_index("groups")
    chip = space // 2
    core = space % 2
    partner = chip * 2 + 1 - core
    across = (1 - chip) * 2 + core
    across_other = (1 - chip) * 2 + 1 - core
    wide = cf + 2
    full = ROW_PAD * frames
    depth = ws_in.shape[1]
    channels = ws_in.shape[2]
    half = depth // 2
    scale = channels ** (-0.5)

    def remote(src, dst, ssem, rsem, where):
        return pltpu.make_async_remote_copy(
            src_ref=src, dst_ref=dst, send_sem=ssem, recv_sem=rsem,
            device_id=where, device_id_type=MESH_ID,
        )

    barrier = pltpu.get_barrier_semaphore()
    for k in range(1, n):
        pl.semaphore_signal(barrier, inc=1, device_id={"space": (space + k) % n}, device_id_type=MESH_ID)
    for k in range(1, frames):
        pl.semaphore_signal(barrier, inc=1, device_id={"frame": (frame + k) % frames}, device_id_type=MESH_ID)
    pl.semaphore_signal(barrier, inc=1, device_id={"groups": 1 - group}, device_id_type=MESH_ID)
    pl.semaphore_wait(barrier, n + frames - 1)

    def p1_copy(which, k):
        source, slab, grow = ((clip_in, clip_slab, 4), (cot_in, cot_slab, 2))[which]
        to = (space + k) % n
        return remote(
            source.at[pl.ds(cs * to, cs + grow)], slab.at[:, space],
            p1_s.at[which, k - 1], p1_r.at[which, k - 1], {"space": to},
        )

    def p1_arrival(which, k):
        slab = (clip_slab, cot_slab)[which]
        came = (space - k + n) % n
        return remote(slab.at[:, came], slab.at[:, came], p1_s.at[which, k - 1], p1_r.at[which, k - 1], {"space": came})

    def p1_local(which):
        source, slab, grow = ((clip_in, clip_slab, 4), (cot_in, cot_slab, 2))[which]
        return pltpu.make_async_copy(source.at[pl.ds(cs * space, cs + grow)], slab.at[:, space], p1_l.at[which])

    sources = (
        [(ws_in, i) for i in range(ws_in.shape[0])]
        + [(wt_in, i) for i in range(wt_in.shape[0])]
        + [(wa_in, i) for i in range(wa_in.shape[0])]
    )
    first_temporal = ws_in.shape[0]
    first_attn = first_temporal + wt_in.shape[0]
    total = len(sources)
    my_rows = pl.ds(pl.multiple_of(group * half, half), half)
    other_rows = pl.ds(pl.multiple_of((1 - group) * half, half), half)

    def x_copy(m):
        ref, i = sources[m]
        return remote(ref.at[i, my_rows], weights.at[m, space, my_rows], x_s.at[m], x_r.at[m], {"space": across})

    def c0_copy(m):
        ref, i = sources[m]
        return remote(ref.at[i], weights.at[m, space], c0_s.at[m], c0_r.at[m], {"space": partner})

    def local_copy(m):
        ref, i = sources[m]
        return pltpu.make_async_copy(ref.at[i], weights.at[m, space], w_loc.at[m])

    for which in range(2):
        for k in range(1, n):
            p1_copy(which, k).start()
        p1_local(which).start()
    for m in range(total):
        x_copy(m).start()
        c0_copy(m).start()
        local_copy(m).start()

    def y_copy(m):
        piece = weights.at[m, across, my_rows]
        return remote(piece, piece, y_s.at[m], y_r.at[m], {"groups": 1 - group})

    def c1_copy(m):
        piece = weights.at[m, across, my_rows]
        return remote(piece, piece, c1_s.at[m], c1_r.at[m], {"space": partner})

    def c2_copy(m):
        piece = weights.at[m, across, other_rows]
        return remote(piece, piece, c2_s.at[m], c2_r.at[m], {"space": partner})

    def arrival(m, owner, rows, ssem, rsem, where):
        piece = weights.at[m, owner, rows] if rows is not None else weights.at[m, owner]
        return remote(piece, piece, ssem.at[m], rsem.at[m], where)

    def relay_first(m):
        arrival(m, across, my_rows, x_s, x_r, {"space": across}).wait_recv()
        y_copy(m).start()
        c1_copy(m).start()

    def relay_second(m):
        arrival(m, across, other_rows, y_s, y_r, {"groups": 1 - group}).wait_recv()
        c2_copy(m).start()

    def ready(m):
        arrival(m, partner, None, c0_s, c0_r, {"space": partner}).wait_recv()
        arrival(m, across_other, my_rows, c1_s, c1_r, {"space": partner}).wait_recv()
        arrival(m, across_other, other_rows, c2_s, c2_r, {"space": partner}).wait_recv()

    def compact(which):
        slab, comp = ((clip_slab, clip_comp), (cot_slab, cot_comp))[which]
        for k in range(1, n):
            p1_arrival(which, k).wait_recv()
        p1_local(which).wait()

        @pl.loop(0, slab.shape[0])
        def _(col):
            rows = jnp.concatenate([slab[col, t].astype(WIDE) for t in range(n)], 0).astype(LOW)
            comp[col] = dot_plain(pick[...], rows).astype(LOW)

    def p2_copy(which, k):
        comp, whole, grow = ((clip_comp, clip_all, 4), (cot_comp, cot_all, 2))[which]
        to = (frame + k) % frames
        return remote(
            comp.at[pl.ds(cf * to, cf + grow)], whole.at[:, frame],
            p2_s.at[which, k - 1], p2_r.at[which, k - 1], {"frame": to},
        )

    def p2_arrival(which, k):
        whole = (clip_all, cot_all)[which]
        came = (frame - k + frames) % frames
        return remote(whole.at[:, came], whole.at[:, came], p2_s.at[which, k - 1], p2_r.at[which, k - 1], {"frame": came})

    def p2_local(which):
        comp, whole, grow = ((clip_comp, clip_all, 4), (cot_comp, cot_all, 2))[which]
        return pltpu.make_async_copy(comp.at[pl.ds(cf * frame, cf + grow)], whole.at[:, frame], p2_l.at[which])

    for which in range(2):
        compact(which)
        for k in range(1, frames):
            p2_copy(which, k).start()
        p2_local(which).start()

    act_pad[:, 0:2] = jnp.zeros((wide, 2, ROW_PAD, channels), LOW)
    glow_pad[:, frames : frames + 2] = jnp.zeros((wide, 2, ROW_PAD, channels), LOW)
    for k in range(1, frames):
        p2_arrival(0, k).wait_recv()
    p2_local(0).wait()

    @pl.loop(0, wide + 2)
    def _(col):
        x = clip_all[col].reshape(full, channels).astype(WIDE)
        inverse = lax.rsqrt(jnp.mean(x * x, -1, keepdims=True) + NORM_EPSILON)
        h = x * inverse * gain[...]
        shifted[0, col] = pltpu.roll(h, 1, 0).astype(LOW)
        shifted[1, col] = h.astype(LOW)
        shifted[2, col] = pltpu.roll(h, full - 1, 0).astype(LOW)

    pre[...] = jnp.zeros_like(pre)
    for m in range(total):
        local_copy(m).wait()

    def weight(m):
        return weights[m].reshape(n * depth, channels)

    relay_first(0)

    @pl.loop(0, taps_total)
    def _(m):
        relay_first(m + 1)
        relay_second(m)
        ready(m)
        lhs = shifted[m // 3, pl.ds(m % 3, wide)].reshape(wide * full, channels)
        pre[...] += dot_plain(lhs, weight(m))

    for m in range(taps_total + 1, total):
        relay_first(m)
    for m in range(taps_total, total):
        relay_second(m)

    @pl.loop(0, wide)
    def _(col):
        p = pre[pl.ds(col * full, full)]
        act_pad[col, pl.ds(2, frames)] = (p * jax.nn.sigmoid(p)).astype(LOW).reshape(frames, ROW_PAD, channels)

    for k in range(1, frames):
        p2_arrival(1, k).wait_recv()
    p2_local(1).wait()
    for m in range(taps_total, total):
        ready(m)

    def flat(ref, lo, count):
        return ref[pl.ds(lo, count)].reshape(count * full, channels)

    mixed = flat(clip_all, 1, wide).astype(WIDE)
    for k in range(wt_in.shape[0]):
        mixed += dot_plain(
            act_pad[:, pl.ds(2 - k, frames)].reshape(wide * full, channels), weight(first_temporal + k)
        )
    low = mixed.astype(LOW)
    resid[...] = low.reshape(resid.shape)

    @pl.loop(0, 3)
    def _(i):
        qs[i] = dot_plain(flat(resid, 0, wide), weight(first_attn + i)).astype(LOW).reshape(resid.shape)

    gs[...] = dot_back(flat(cot_all, 0, wide), weight(first_attn + 3)).astype(LOW).reshape(resid.shape)

    @pl.loop(0, wide)
    def _(col):
        q = [qs[0, col, f].astype(WIDE) for f in range(frames)]
        kk = [qs[1, col, f].astype(WIDE) for f in range(frames)]
        v = [qs[2, col, f].astype(WIDE) for f in range(frames)]
        up = [gs[col, f].astype(WIDE) for f in range(frames)]
        gk = [None] * frames
        gv = [None] * frames
        for f in range(frames):
            sc = [
                jnp.sum(q[f] * kk[g], -1, keepdims=True) * scale + bias[col, f * frames + g][:, :1]
                for g in range(f + 1)
            ]
            top = sc[0]
            for g in range(1, f + 1):
                top = jnp.maximum(top, sc[g])
            ex = [jnp.exp(s - top) for s in sc]
            den = ex[0]
            for g in range(1, f + 1):
                den = den + ex[g]
            pr = [e / den for e in ex]
            gp = [jnp.sum(up[f] * v[g], -1, keepdims=True) for g in range(f + 1)]
            dot_sum = pr[0] * gp[0]
            for g in range(1, f + 1):
                dot_sum = dot_sum + pr[g] * gp[g]
            a = None
            gq = None
            for g in range(f + 1):
                pl_low = pr[g].astype(LOW).astype(WIDE)
                sg = (pr[g] * (gp[g] - dot_sum)).astype(LOW).astype(WIDE)
                a = pl_low * v[g] if a is None else a + pl_low * v[g]
                gq = sg * kk[g] if gq is None else gq + sg * kk[g]
                tk = (sg * q[f] * scale).astype(LOW).astype(WIDE)
                tv = (pl_low * up[f]).astype(LOW).astype(WIDE)
                gk[g] = tk if gk[g] is None else gk[g] + tk
                gv[g] = tv if gv[g] is None else gv[g] + tv
            att[col, f] = a.astype(LOW)
            ks[0, col, f] = (gq * scale).astype(LOW)
        for g in range(frames):
            ks[1, col, g] = gk[g].astype(LOW)
            ks[2, col, g] = gv[g].astype(LOW)

    def spread(own, values):
        for c in range(cf):
            own[:, c] = values[c * full : (c + 1) * full].astype(LOW).reshape(frames, ROW_PAD, channels)

    block = flat(resid, 1, cf).astype(WIDE) + dot_plain(flat(att, 1, cf), weight(first_attn + 3))
    spread(block_own, block)

    def oz_copy(which, k):
        own, z = ((block_own, block_z), (grad_own, grad_z))[which]
        to = (frame + k) % frames
        return remote(own.at[to], z.at[frame], oz_s.at[which, k - 1], oz_r.at[which, k - 1], {"frame": to})

    def oz_arrival(which, k):
        z = (block_z, grad_z)[which]
        came = (frame - k + frames) % frames
        return remote(z.at[came], z.at[came], oz_s.at[which, k - 1], oz_r.at[which, k - 1], {"frame": came})

    def oz_local(which):
        own, z = ((block_own, block_z), (grad_own, grad_z))[which]
        return pltpu.make_async_copy(own.at[frame], z.at[frame], oz_l.at[which])

    def ox_copy(which, k):
        slab, out = ((block_slab, out_block), (grad_slab, out_grad))[which]
        to = (space + k) % n
        return remote(
            slab.at[to], out.at[pl.ds(cs * space, cs)], ox_s.at[which, k - 1], ox_r.at[which, k - 1], {"space": to}
        )

    def ox_arrival(which, k):
        out = (out_block, out_grad)[which]
        came = (space - k + n) % n
        piece = out.at[pl.ds(cs * came, cs)]
        return remote(piece, piece, ox_s.at[which, k - 1], ox_r.at[which, k - 1], {"space": came})

    def ox_local(which):
        slab, out = ((block_slab, out_block), (grad_slab, out_grad))[which]
        return pltpu.make_async_copy(slab.at[space], out.at[pl.ds(cs * space, cs)], ox_l.at[which])

    def send_frames(which):
        for k in range(1, frames):
            oz_copy(which, k).start()
        oz_local(which).start()

    def send_tiles(which):
        z, slab = ((block_z, block_slab), (grad_z, grad_slab))[which]
        for k in range(1, frames):
            oz_arrival(which, k).wait_recv()
        oz_local(which).wait()

        @pl.loop(0, frames)
        def _(f):
            for c in range(cf):
                rows = dot_plain(place[...], z[f, c])
                for t in range(n):
                    slab[t, f * cf + c] = rows[t * SLOT_PAD : (t + 1) * SLOT_PAD].astype(LOW)

        for k in range(1, n):
            ox_copy(which, k).start()
        ox_local(which).start()

    send_frames(0)
    gres[...] = flat(cot_all, 0, wide).astype(WIDE)

    @pl.loop(0, 3)
    def _(i):
        gres[...] += dot_back(flat(ks.at[i], 0, wide), weight(first_attn + i))

    glow_pad[:, pl.ds(0, frames)] = gres[...].astype(LOW).reshape(resid.shape)
    send_tiles(0)
    gact = None
    for k in range(wt_in.shape[0]):
        term = dot_back(glow_pad[:, pl.ds(k, frames)].reshape(wide * full, channels), weight(first_temporal + k))
        gact = term if gact is None else gact + term
    pre_all = pre[...]
    sig = jax.nn.sigmoid(pre_all)
    pre[...] = gact * sig * (1.0 + pre_all * (1.0 - sig))

    @pl.loop(0, wide)
    def _(col):
        p = jnp.where(keep[col][:, :1] > 0.5, pre[pl.ds(col * full, full)], 0.0)
        shifted[0, col] = pltpu.roll(p, 1, 0).astype(LOW)
        shifted[1, col] = p.astype(LOW)
        shifted[2, col] = pltpu.roll(p, full - 1, 0).astype(LOW)

    ghid[...] = jnp.zeros_like(ghid)

    @pl.loop(0, taps_total)
    def _(m):
        lhs = shifted[2 - m // 3, pl.ds(2 - m % 3, cf)].reshape(cf * full, channels)
        ghid[...] += dot_back(lhs, weight(m))

    for c in range(cf):
        x = clip_all[c + 2].reshape(full, channels).astype(WIDE)
        inverse = lax.rsqrt(jnp.mean(x * x, -1, keepdims=True) + NORM_EPSILON)
        normed = x * inverse
        gn = ghid[c * full : (c + 1) * full] * gain[...]
        back = inverse * (gn - normed * jnp.mean(gn * normed, -1, keepdims=True))
        result = gres[(c + 1) * full : (c + 2) * full] + back
        grad_own[:, c] = result.astype(LOW).reshape(frames, ROW_PAD, channels)

    send_frames(1)
    send_tiles(1)
    for which in range(2):
        for k in range(1, n):
            ox_arrival(which, k).wait_recv()
        ox_local(which).wait()
        for k in range(1, n):
            p1_copy(which, k).wait_send()
            ox_copy(which, k).wait_send()
        for k in range(1, frames):
            p2_copy(which, k).wait_send()
            oz_copy(which, k).wait_send()
    for m in range(total):
        x_copy(m).wait_send()
        c0_copy(m).wait_send()
        y_copy(m).wait_send()
        c1_copy(m).wait_send()
        c2_copy(m).wait_send()


def per_device_strips(clip, cotangent, tile_rows, frame_start, norm_gain, w_spatial, w_temporal, w_attn):
    slots = clip.shape[1]
    breadth = clip.shape[2]
    channels = clip.shape[3]
    n = lax.axis_size("space")
    frames = lax.axis_size("frame")
    space = lax.axis_index("space")
    frame = lax.axis_index("frame")
    cs = breadth // n
    cf = cs // frames
    wide = cf + 2
    full = ROW_PAD * frames
    depth = w_spatial.shape[1]
    taps_total = w_spatial.shape[0]
    total = taps_total + w_temporal.shape[0] + w_attn.shape[0]
    bounds = jnp.cumsum(tile_rows) - tile_rows
    slot_ids = jnp.arange(SLOT_PAD)
    row_of = jnp.where(slot_ids[None, :] < tile_rows[:, None], bounds[:, None] + slot_ids[None, :], -1).reshape(-1)
    place = (row_of[:, None] == jnp.arange(ROW_PAD)[None, :]).astype(LOW)
    pick = (row_of[None, :] == jnp.arange(ROW_PAD)[:, None]).astype(LOW)
    columns = space * cs + frame * cf - 1 + jnp.arange(wide)
    inside = (columns >= 0) & (columns < breadth)
    starts = jnp.take(frame_start, jnp.clip(columns, 0, breadth - 1), axis=1)
    bias = jnp.where(starts.T[:, :, None] <= jnp.arange(frames)[None, None, :], 0.0, -1e30).astype(WIDE)
    bias = jnp.broadcast_to(bias.reshape(wide, frames * frames, 1, 1), (wide, frames * frames, 1, 128))
    live_row = (jnp.arange(full) % ROW_PAD) < jnp.sum(tile_rows)
    keep = jnp.broadcast_to(
        (inside[:, None] & live_row[None, :]).astype(WIDE)[:, :, None], (wide, full, 128)
    )
    def by_column(values, halo):
        turned = jnp.transpose(values[0], (1, 0, 2))
        return jnp.pad(turned, ((halo, halo), (0, SLOT_PAD - slots), (0, 0)))

    vmem = pl.BlockSpec(memory_space=pltpu.VMEM)
    hbm = pl.BlockSpec(memory_space=pl.ANY)
    dma = pltpu.SemaphoreType.DMA
    shape4 = (frames, ROW_PAD, channels)
    scratch = [
        pltpu.VMEM((total, n, depth, channels), LOW),
        pltpu.VMEM((cs + 4, n, SLOT_PAD, channels), LOW),
        pltpu.VMEM((cs + 2, n, SLOT_PAD, channels), LOW),
        pltpu.VMEM((cs + 4, ROW_PAD, channels), LOW),
        pltpu.VMEM((cs + 2, ROW_PAD, channels), LOW),
        pltpu.VMEM((wide + 2,) + shape4, LOW),
        pltpu.VMEM((wide,) + shape4, LOW),
        pltpu.VMEM((3, wide + 2, full, channels), LOW),
        pltpu.VMEM((wide * full, channels), WIDE),
        pltpu.VMEM((wide, frames + 2, ROW_PAD, channels), LOW),
        pltpu.VMEM((wide,) + shape4, LOW),
        pltpu.VMEM((3, wide) + shape4, LOW),
        pltpu.VMEM((3, wide) + shape4, LOW),
        pltpu.VMEM((wide,) + shape4, LOW),
        pltpu.VMEM((wide,) + shape4, LOW),
        pltpu.VMEM((wide * full, channels), WIDE),
        pltpu.VMEM((wide, frames + 2, ROW_PAD, channels), LOW),
        pltpu.VMEM((cf * full, channels), WIDE),
        pltpu.VMEM((frames, cf, ROW_PAD, channels), LOW),
        pltpu.VMEM((frames, cf, ROW_PAD, channels), LOW),
        pltpu.VMEM((frames, cf, ROW_PAD, channels), LOW),
        pltpu.VMEM((frames, cf, ROW_PAD, channels), LOW),
        pltpu.VMEM((n, cs, SLOT_PAD, channels), LOW),
        pltpu.VMEM((n, cs, SLOT_PAD, channels), LOW),
    ]
    scratch += [dma((total,)) for _ in range(11)]
    scratch += [dma((2, n - 1)), dma((2, n - 1)), dma((2,))]
    scratch += [dma((2, frames - 1)), dma((2, frames - 1)), dma((2,))] * 2
    scratch += [dma((2, n - 1)), dma((2, n - 1)), dma((2,))]
    out = jax.ShapeDtypeStruct((breadth, SLOT_PAD, channels), LOW)
    block, grad = pl.pallas_call(
        functools.partial(strip_kernel, n, frames, cs, cf, taps_total),
        out_shape=(out, out),
        in_specs=[vmem] * 5 + [hbm] * 5,
        out_specs=(vmem, vmem),
        scratch_shapes=scratch,
        compiler_params=pltpu.CompilerParams(
            collective_id=0, has_side_effects=True, vmem_limit_bytes=48 * 1024 * 1024
        ),
    )(
        pick, place, norm_gain.reshape(1, channels), bias, keep,
        by_column(clip, 2), by_column(cotangent, 1), w_spatial, w_temporal, w_attn,
    )

    def by_slot(values):
        return jnp.transpose(values[:, :slots], (1, 0, 2))[None]

    return by_slot(block), by_slot(grad)


def strips_fit(mesh, clip, tile_rows):
    n = mesh.shape["space"]
    frames = mesh.shape["frame"]
    slots_all, breadth, channels = clip.shape[1:]
    return (
        mesh.shape["groups"] == 2
        and n == 4
        and breadth % (n * frames) == 0
        and slots_all // n <= SLOT_PAD
        and slots_all // 2 < ROW_PAD
        and channels % (128 * n) == 0
    )


def solution(mesh):
    placed = (
        P(("groups", "frame"), "space", None, None),
        P(("groups", "frame"), "space", None, None),
        P("groups"),
        P("groups", None),
        P(),
        P(None, "space", None),
        P(None, "space", None),
        P(None, "space", None),
    )

    def run(*arrays):
        fits = strips_fit(mesh, arrays[0], arrays[2])
        return jax.shard_map(
            per_device_strips if fits else per_device,
            mesh=mesh,
            in_specs=placed,
            out_specs=(
                P(("groups", "frame"), "space", None, None),
                P(("groups", "frame"), "space", None, None),
            ),
            check_vma=False,
        )(*arrays)

    return run
```

```python
import functools

import jax
import jax.numpy as jnp
from jax import lax
from jax.experimental import pallas as pl
from jax.experimental.pallas import tpu as pltpu
from jax.sharding import PartitionSpec as P

NORM_EPSILON = 1e-06


def passed_along(value, axis, steps):
    count = lax.axis_size(axis)
    first, last = (max(0, -steps), min(count, count - steps))
    return lax.ppermute(value, axis, [(source, source + steps) for source in range(first, last)])


def tile_rim(edge_row, offset):
    return passed_along(edge_row, "space", offset)


def frame_rim(values, offset):
    return passed_along(values, "frame", offset)


def with_faces(values, row_count):
    height = values.shape[0]
    lowest = lax.dynamic_index_in_dim(values, row_count - 1, 0, keepdims=False)
    upper_face = tile_rim(lowest, 1)
    lower_face = tile_rim(values[0], -1)
    extended = jnp.concatenate([upper_face[None], values, jnp.zeros_like(values[:1])], 0)
    position = lax.broadcasted_iota(jnp.int32, (height + 2, 1, 1), 0)
    extended = jnp.where(position == row_count + 1, lower_face[None], extended)
    return jnp.pad(extended, ((0, 0), (1, 1), (0, 0)))


def spatial_conv(extended, kernel, flipped):
    height = extended.shape[0] - 2
    breadth = extended.shape[1] - 2
    summed = None
    for tap_row in range(3):
        for tap_col in range(3):
            patches = extended[tap_row : tap_row + height, tap_col : tap_col + breadth]
            if flipped:
                product = jnp.einsum(
                    "hwd,ed->hwe",
                    patches,
                    kernel[(2 - tap_row) * 3 + 2 - tap_col],
                    preferred_element_type=jnp.float32,
                )
            else:
                product = jnp.einsum(
                    "hwd,de->hwe",
                    patches,
                    kernel[tap_row * 3 + tap_col],
                    preferred_element_type=jnp.float32,
                )
            summed = product if summed is None else summed + product
    return summed


def project(values, matrix):
    return jnp.einsum("hwd,de->hwe", values, matrix, preferred_element_type=jnp.float32)


def project_back(values, matrix):
    return jnp.einsum("hwe,de->hwd", values, matrix, preferred_element_type=jnp.float32)


def per_device(clip, cotangent, tile_rows, frame_start, norm_gain, w_spatial, w_temporal, w_attn):
    height = clip.shape[1]
    breadth = clip.shape[2]
    channels = clip.shape[3]
    frames = lax.axis_size("frame")
    frame_now = lax.axis_index("frame")
    row_count = tile_rows[lax.axis_index("space")]
    live = (lax.broadcasted_iota(jnp.int32, (height, 1, 1), 0) < row_count).astype(jnp.float32)
    score_scale = channels ** (-0.5)
    kernel, temporal, attention = (
        lax.all_gather(w_spatial, "space", axis=1, tiled=True),
        lax.all_gather(w_temporal, "space", axis=1, tiled=True),
        lax.all_gather(w_attn, "space", axis=1, tiled=True),
    )
    inputs = clip[0].astype(jnp.float32)
    inverse = lax.rsqrt(jnp.mean(inputs * inputs, -1, keepdims=True) + NORM_EPSILON)
    normed = inputs * inverse
    hidden = (normed * norm_gain * live).astype(jnp.bfloat16)
    preact = spatial_conv(with_faces(hidden, row_count), kernel, False) * live
    activated = jax.nn.silu(preact).astype(jnp.bfloat16)
    mixed = (
        project(activated, temporal[0])
        + project(frame_rim(activated, 1), temporal[1])
        + project(frame_rim(activated, 2), temporal[2])
    )
    residual = ((inputs + mixed) * live).astype(jnp.bfloat16)
    queries = project(residual, attention[0]).astype(jnp.bfloat16)
    keys_own = project(residual, attention[1]).astype(jnp.bfloat16)
    values_own = project(residual, attention[2]).astype(jnp.bfloat16)
    upstream = cotangent[0].astype(jnp.float32) * live
    grad_out = upstream.astype(jnp.bfloat16)
    grad_attended = project_back(grad_out, attention[3]).astype(jnp.bfloat16)
    pixels = height * breadth
    share = pixels // frames
    outgoing = jnp.stack(
        [
            queries.reshape(1, pixels, channels),
            keys_own.reshape(1, pixels, channels),
            values_own.reshape(1, pixels, channels),
            grad_attended.reshape(1, pixels, channels),
        ]
    )
    arrived = lax.all_to_all(outgoing, "frame", split_axis=2, concat_axis=1, tiled=True)
    query_all = arrived[0]
    key_all = arrived[1]
    value_all = arrived[2]
    upward_all = arrived[3]
    frame_ids = lax.iota(jnp.int32, frames)
    columns = (frame_now * share + lax.iota(jnp.int32, share)) % breadth
    starts = jnp.take(frame_start, columns, axis=1)
    allowed = (frame_ids[None, :, None] >= starts[:, None, :]) & (
        frame_ids[None, :, None] <= frame_ids[:, None, None]
    )
    scores = (
        jnp.einsum("fpc,gpc->fgp", query_all, key_all, preferred_element_type=jnp.float32)
        * score_scale
    )
    scores = jnp.where(allowed, scores, -jnp.inf)
    probs = jax.nn.softmax(scores, axis=1)
    probs_low = probs.astype(jnp.bfloat16)
    attended_all = jnp.einsum(
        "fgp,gpc->fpc", probs_low, value_all, preferred_element_type=jnp.float32
    ).astype(jnp.bfloat16)
    grad_probs = jnp.einsum(
        "fpc,gpc->fgp", upward_all, value_all, preferred_element_type=jnp.float32
    )
    grad_scores = probs * (grad_probs - jnp.sum(probs * grad_probs, 1, keepdims=True))
    grad_scores_low = grad_scores.astype(jnp.bfloat16)
    grad_query_all = (
        jnp.einsum("fgp,gpc->fpc", grad_scores_low, key_all, preferred_element_type=jnp.float32)
        * score_scale
    ).astype(jnp.bfloat16)
    key_terms = (
        jnp.einsum("fgp,fpc->fgpc", grad_scores_low, query_all, preferred_element_type=jnp.float32)
        * score_scale
    ).astype(jnp.bfloat16)
    grad_key_all = jnp.sum(key_terms.astype(jnp.float32), 0).astype(jnp.bfloat16)
    value_terms = jnp.einsum(
        "fgp,fpc->fgpc", probs_low, upward_all, preferred_element_type=jnp.float32
    ).astype(jnp.bfloat16)
    grad_value_all = jnp.sum(value_terms.astype(jnp.float32), 0).astype(jnp.bfloat16)
    returning = jnp.stack([attended_all, grad_query_all, grad_key_all, grad_value_all])
    came_back = lax.all_to_all(returning, "frame", split_axis=1, concat_axis=2, tiled=True)
    attended = came_back[0, 0].reshape(height, breadth, channels)
    grad_queries = came_back[1, 0].reshape(height, breadth, channels)
    grad_keys_low = came_back[2, 0].reshape(height, breadth, channels)
    grad_values_low = came_back[3, 0].reshape(height, breadth, channels)
    block_output = ((residual.astype(jnp.float32) + project(attended, attention[3])) * live).astype(
        jnp.bfloat16
    )
    grad_resid = (
        upstream
        + project_back(grad_queries, attention[0])
        + project_back(grad_keys_low, attention[1])
        + project_back(grad_values_low, attention[2])
    )
    grad_resid = grad_resid * live
    grad_low = grad_resid.astype(jnp.bfloat16)
    grad_act = (
        project_back(grad_low, temporal[0])
        + project_back(frame_rim(grad_low, -1), temporal[1])
        + project_back(frame_rim(grad_low, -2), temporal[2])
    )
    sigmoid_pre = jax.nn.sigmoid(preact)
    grad_pre = (grad_act * sigmoid_pre * (1.0 + preact * (1.0 - sigmoid_pre)) * live).astype(
        jnp.bfloat16
    )
    grad_hidden = spatial_conv(with_faces(grad_pre, row_count), kernel, True)
    grad_normed = grad_hidden * norm_gain
    grad_inputs = inverse * (
        grad_normed - normed * jnp.mean(grad_normed * normed, -1, keepdims=True)
    )
    clip_grad = ((grad_resid + grad_inputs) * live).astype(jnp.bfloat16)
    return (block_output[None], clip_grad[None])


MESH_ID = pl.DeviceIdType.MESH
LOW = jnp.bfloat16
WIDE = jnp.float32
ROW_PAD = 16
SLOT_PAD = 8


def dot_plain(left, right):
    return jnp.dot(left, right, preferred_element_type=WIDE)


def dot_back(left, right):
    return lax.dot_general(left, right, (((1,), (1,)), ((), ())), preferred_element_type=WIDE)


def strip_kernel(
    n, frames, cs, cf, taps_total,
    rows_in, starts_in, gain, clip_in, cot_in, ws_in, wt_in, wa_in,
    out_block, out_grad,
    weights, clip_slab, cot_slab, clip_comp, cot_comp, clip_all, cot_all,
    shifted, pre, act_pad, resid, qs, ks, gs, att, gres, glow_pad, ghid,
    block_own, grad_own, block_z, grad_z, block_slab, grad_slab,
    x_s, x_r, c0_s, c0_r, y_s, y_r, c1_s, c1_r, c2_s, c2_r,
    z_s, z_r, yd_s, yd_r, zd_s, zd_r, c3_s, c3_r, c4_s, c4_r, w_loc,
    p1_s, p1_r, p1_l, p2_s, p2_r, p2_l, oz_s, oz_r, oz_l, ox_s, ox_r, ox_l,
):
    space = lax.axis_index("space")
    frame = lax.axis_index("frame")
    group = lax.axis_index("groups")
    chip = space // 2
    core = space % 2
    partner = chip * 2 + 1 - core
    across = (1 - chip) * 2 + core
    across_other = (1 - chip) * 2 + 1 - core
    wide = cf + 2
    full = ROW_PAD * frames
    depth = ws_in.shape[1]
    channels = ws_in.shape[2]
    half = depth // 2
    scale = channels ** (-0.5)

    def remote(src, dst, ssem, rsem, where):
        return pltpu.make_async_remote_copy(
            src_ref=src, dst_ref=dst, send_sem=ssem, recv_sem=rsem,
            device_id=where, device_id_type=MESH_ID,
        )

    bound = 0
    bounds = []
    for t in range(n):
        bounds.append(bound)
        bound = bound + rows_in[t]

    def selection(shape, slot_dim):
        slot = lax.broadcasted_iota(jnp.int32, shape, slot_dim)
        row = lax.broadcasted_iota(jnp.int32, shape, 1 - slot_dim)
        chosen = jnp.zeros(shape, WIDE)
        for t in range(n):
            offset = slot - t * SLOT_PAD
            hit = (offset >= 0) & (offset < rows_in[t]) & (row == offset + bounds[t])
            chosen = jnp.where(hit, 1.0, chosen)
        return chosen.astype(LOW)

    first_column = space * cs + frame * cf - 1

    barrier = pltpu.get_barrier_semaphore()
    for k in range(1, n):
        pl.semaphore_signal(barrier, inc=1, device_id={"space": (space + k) % n}, device_id_type=MESH_ID)
    for k in range(1, frames):
        pl.semaphore_signal(barrier, inc=1, device_id={"frame": (frame + k) % frames}, device_id_type=MESH_ID)
    pl.semaphore_signal(barrier, inc=1, device_id={"groups": 1 - group}, device_id_type=MESH_ID)
    pl.semaphore_wait(barrier, n + frames - 1)

    def p1_copy(which, k):
        source, slab, grow = ((clip_in, clip_slab, 4), (cot_in, cot_slab, 2))[which]
        to = (space + k) % n
        return remote(
            source.at[pl.ds(cs * to, cs + grow)], slab.at[:, space],
            p1_s.at[which, k - 1], p1_r.at[which, k - 1], {"space": to},
        )

    def p1_arrival(which, k):
        slab = (clip_slab, cot_slab)[which]
        came = (space - k + n) % n
        return remote(slab.at[:, came], slab.at[:, came], p1_s.at[which, k - 1], p1_r.at[which, k - 1], {"space": came})

    def p1_local(which):
        source, slab, grow = ((clip_in, clip_slab, 4), (cot_in, cot_slab, 2))[which]
        return pltpu.make_async_copy(source.at[pl.ds(cs * space, cs + grow)], slab.at[:, space], p1_l.at[which])

    sources = (
        [(ws_in, i) for i in range(ws_in.shape[0])]
        + [(wt_in, i) for i in range(wt_in.shape[0])]
        + [(wa_in, i) for i in range(wa_in.shape[0])]
    )
    first_temporal = ws_in.shape[0]
    first_attn = first_temporal + wt_in.shape[0]
    total = len(sources)
    my_rows = pl.ds(pl.multiple_of(group * half, half), half)
    other_rows = pl.ds(pl.multiple_of((1 - group) * half, half), half)

    z_bit = frame % 2
    peer = {"frame": frame + 1 - 2 * z_bit}
    q_me = 2 * group + z_bit
    q_y = 2 * (1 - group) + z_bit
    q_z = 2 * group + 1 - z_bit
    q_d = 2 * (1 - group) + 1 - z_bit
    part = depth // 4

    def quarter(q):
        return pl.ds(pl.multiple_of(q * part, part), part)

    def eighth(q, second):
        return pl.ds(pl.multiple_of(q * part + second * (part // 2), part // 2), part // 2)

    def x_copy(m):
        ref, i = sources[m]
        rows = my_rows if m < taps_total else quarter(q_me)
        return remote(ref.at[i, rows], weights.at[m, space, rows], x_s.at[m], x_r.at[m], {"space": across})

    def c0_copy(m):
        ref, i = sources[m]
        return remote(ref.at[i], weights.at[m, space], c0_s.at[m], c0_r.at[m], {"space": partner})

    def local_copy(m):
        ref, i = sources[m]
        return pltpu.make_async_copy(ref.at[i], weights.at[m, space], w_loc.at[m])

    for which in range(2):
        for k in range(1, n):
            p1_copy(which, k).start()
        p1_local(which).start()
    for m in range(total):
        x_copy(m).start()
        c0_copy(m).start()
        local_copy(m).start()

    def y_copy(m):
        piece = weights.at[m, across, my_rows]
        return remote(piece, piece, y_s.at[m], y_r.at[m], {"groups": 1 - group})

    def c1_copy(m):
        piece = weights.at[m, across, my_rows]
        return remote(piece, piece, c1_s.at[m], c1_r.at[m], {"space": partner})

    def c2_copy(m):
        piece = weights.at[m, across, other_rows]
        return remote(piece, piece, c2_s.at[m], c2_r.at[m], {"space": partner})

    def arrival(m, owner, rows, ssem, rsem, where):
        piece = weights.at[m, owner, rows] if rows is not None else weights.at[m, owner]
        return remote(piece, piece, ssem.at[m], rsem.at[m], where)

    def relay_first(m):
        arrival(m, across, my_rows, x_s, x_r, {"space": across}).wait_recv()
        y_copy(m).start()
        c1_copy(m).start()

    def relay_second(m):
        arrival(m, across, other_rows, y_s, y_r, {"groups": 1 - group}).wait_recv()
        c2_copy(m).start()

    def ready(m):
        arrival(m, partner, None, c0_s, c0_r, {"space": partner}).wait_recv()
        arrival(m, across_other, my_rows, c1_s, c1_r, {"space": partner}).wait_recv()
        arrival(m, across_other, other_rows, c2_s, c2_r, {"space": partner}).wait_recv()

    flip = {"groups": 1 - group}
    home = {"space": partner}

    def quad_copy(m, rows, ssem, rsem, where):
        piece = weights.at[m, across, rows]
        return remote(piece, piece, ssem.at[m], rsem.at[m], where)

    def quad_sends(m):
        return (
            quad_copy(m, quarter(q_me), y_s, y_r, flip),
            quad_copy(m, quarter(q_me), z_s, z_r, peer),
            quad_copy(m, quarter(q_me), c1_s, c1_r, home),
            quad_copy(m, eighth(q_y, 0), zd_s, zd_r, peer),
            quad_copy(m, quarter(q_y), c2_s, c2_r, home),
            quad_copy(m, eighth(q_z, 1), yd_s, yd_r, flip),
            quad_copy(m, quarter(q_z), c3_s, c3_r, home),
            quad_copy(m, quarter(q_d), c4_s, c4_r, home),
        )

    def quad_first(m):
        arrival(m, across, quarter(q_me), x_s, x_r, {"space": across}).wait_recv()
        for copy in quad_sends(m)[0:3]:
            copy.start()

    def quad_second(m):
        arrival(m, across, quarter(q_y), y_s, y_r, flip).wait_recv()
        for copy in quad_sends(m)[3:5]:
            copy.start()
        arrival(m, across, quarter(q_z), z_s, z_r, peer).wait_recv()
        for copy in quad_sends(m)[5:7]:
            copy.start()

    def quad_third(m):
        arrival(m, across, eighth(q_d, 0), zd_s, zd_r, peer).wait_recv()
        arrival(m, across, eighth(q_d, 1), yd_s, yd_r, flip).wait_recv()
        quad_sends(m)[7].start()

    def quad_ready(m):
        arrival(m, partner, None, c0_s, c0_r, home).wait_recv()
        arrival(m, across_other, quarter(q_me), c1_s, c1_r, home).wait_recv()
        arrival(m, across_other, quarter(q_y), c2_s, c2_r, home).wait_recv()
        arrival(m, across_other, quarter(q_z), c3_s, c3_r, home).wait_recv()
        arrival(m, across_other, quarter(q_d), c4_s, c4_r, home).wait_recv()

    reached = [taps_total, taps_total, taps_total, taps_total]

    def advance(m):
        for step, ahead, act in ((0, 2, quad_first), (1, 1, quad_second), (2, 0, quad_third), (3, 0, quad_ready)):
            while reached[step] <= min(m + ahead, total - 1):
                act(reached[step])
                reached[step] += 1

    def compact(which):
        slab, comp = ((clip_slab, clip_comp), (cot_slab, cot_comp))[which]
        for k in range(1, n):
            p1_arrival(which, k).wait_recv()
        p1_local(which).wait()

        @pl.loop(0, slab.shape[0])
        def _(col):
            rows = jnp.concatenate([slab[col, t].astype(WIDE) for t in range(n)], 0).astype(LOW)
            comp[col] = dot_plain(pick, rows).astype(LOW)

    def p2_copy(which, k):
        comp, whole, grow = ((clip_comp, clip_all, 4), (cot_comp, cot_all, 2))[which]
        to = (frame + k) % frames
        return remote(
            comp.at[pl.ds(cf * to, cf + grow)], whole.at[:, frame],
            p2_s.at[which, k - 1], p2_r.at[which, k - 1], {"frame": to},
        )

    def p2_arrival(which, k):
        whole = (clip_all, cot_all)[which]
        came = (frame - k + frames) % frames
        return remote(whole.at[:, came], whole.at[:, came], p2_s.at[which, k - 1], p2_r.at[which, k - 1], {"frame": came})

    def p2_local(which):
        comp, whole, grow = ((clip_comp, clip_all, 4), (cot_comp, cot_all, 2))[which]
        return pltpu.make_async_copy(comp.at[pl.ds(cf * frame, cf + grow)], whole.at[:, frame], p2_l.at[which])

    pick = selection((ROW_PAD, n * SLOT_PAD), 1)
    for which in range(2):
        compact(which)
        for k in range(1, frames):
            p2_copy(which, k).start()
        p2_local(which).start()

    act_pad[:, 0:2] = jnp.zeros((wide, 2, ROW_PAD, channels), LOW)
    glow_pad[:, frames : frames + 2] = jnp.zeros((wide, 2, ROW_PAD, channels), LOW)
    for k in range(1, frames):
        p2_arrival(0, k).wait_recv()
    p2_local(0).wait()

    @pl.loop(0, wide + 2)
    def _(col):
        x = clip_all[col].reshape(full, channels).astype(WIDE)
        inverse = lax.rsqrt(jnp.mean(x * x, -1, keepdims=True) + NORM_EPSILON)
        h = x * inverse * gain[...]
        shifted[0, col] = pltpu.roll(h, 1, 0).astype(LOW)
        shifted[1, col] = h.astype(LOW)
        shifted[2, col] = pltpu.roll(h, full - 1, 0).astype(LOW)

    pre[...] = jnp.zeros_like(pre)
    for m in range(total):
        local_copy(m).wait()

    def weight(m):
        return weights[m].reshape(n * depth, channels)

    relay_first(0)

    def tap(m):
        relay_second(m)
        ready(m)
        lhs = shifted[m // 3, pl.ds(m % 3, wide)].reshape(wide * full, channels)
        pre[...] += dot_plain(lhs, weight(m))

    @pl.loop(0, taps_total - 1)
    def _(m):
        relay_first(m + 1)
        tap(m)

    quad_first(taps_total)
    reached[0] += 1
    tap(taps_total - 1)

    @pl.loop(0, wide)
    def _(col):
        p = pre[pl.ds(col * full, full)]
        act_pad[col, pl.ds(2, frames)] = (p * jax.nn.sigmoid(p)).astype(LOW).reshape(frames, ROW_PAD, channels)

    for k in range(1, frames):
        p2_arrival(1, k).wait_recv()
    p2_local(1).wait()

    def flat(ref, lo, count):
        return ref[pl.ds(lo, count)].reshape(count * full, channels)

    mixed = flat(clip_all, 1, wide).astype(WIDE)
    for k in range(wt_in.shape[0]):
        advance(first_temporal + k)
        mixed += dot_plain(
            act_pad[:, pl.ds(2 - k, frames)].reshape(wide * full, channels), weight(first_temporal + k)
        )
    low = mixed.astype(LOW)
    resid[...] = low.reshape(resid.shape)

    for i in range(3):
        advance(first_attn + i)
        qs[i] = dot_plain(flat(resid, 0, wide), weight(first_attn + i)).astype(LOW).reshape(resid.shape)

    advance(first_attn + 3)
    gs[...] = dot_back(flat(cot_all, 0, wide), weight(first_attn + 3)).astype(LOW).reshape(resid.shape)

    @pl.loop(0, wide)
    def _(col):
        q = [qs[0, col, f].astype(WIDE) for f in range(frames)]
        kk = [qs[1, col, f].astype(WIDE) for f in range(frames)]
        v = [qs[2, col, f].astype(WIDE) for f in range(frames)]
        up = [gs[col, f].astype(WIDE) for f in range(frames)]
        gk = [None] * frames
        gv = [None] * frames
        column = jnp.clip(first_column + col, 0, cs * n - 1)
        for f in range(frames):
            start = starts_in[f, column]
            sc = [
                jnp.sum(q[f] * kk[g], -1, keepdims=True) * scale + jnp.where(start <= g, 0.0, -1e30)
                for g in range(f + 1)
            ]
            top = sc[0]
            for g in range(1, f + 1):
                top = jnp.maximum(top, sc[g])
            ex = [jnp.exp(s - top) for s in sc]
            den = ex[0]
            for g in range(1, f + 1):
                den = den + ex[g]
            pr = [e / den for e in ex]
            gp = [jnp.sum(up[f] * v[g], -1, keepdims=True) for g in range(f + 1)]
            dot_sum = pr[0] * gp[0]
            for g in range(1, f + 1):
                dot_sum = dot_sum + pr[g] * gp[g]
            a = None
            gq = None
            for g in range(f + 1):
                pl_low = pr[g].astype(LOW).astype(WIDE)
                sg = (pr[g] * (gp[g] - dot_sum)).astype(LOW).astype(WIDE)
                a = pl_low * v[g] if a is None else a + pl_low * v[g]
                gq = sg * kk[g] if gq is None else gq + sg * kk[g]
                tk = (sg * q[f] * scale).astype(LOW).astype(WIDE)
                tv = (pl_low * up[f]).astype(LOW).astype(WIDE)
                gk[g] = tk if gk[g] is None else gk[g] + tk
                gv[g] = tv if gv[g] is None else gv[g] + tv
            att[col, f] = a.astype(LOW)
            ks[0, col, f] = (gq * scale).astype(LOW)
        for g in range(frames):
            ks[1, col, g] = gk[g].astype(LOW)
            ks[2, col, g] = gv[g].astype(LOW)

    def spread(own, values):
        for c in range(cf):
            own[:, c] = values[c * full : (c + 1) * full].astype(LOW).reshape(frames, ROW_PAD, channels)

    block = flat(resid, 1, cf).astype(WIDE) + dot_plain(flat(att, 1, cf), weight(first_attn + 3))
    spread(block_own, block)

    def oz_copy(which, k):
        own, z = ((block_own, block_z), (grad_own, grad_z))[which]
        to = (frame + k) % frames
        return remote(own.at[to], z.at[frame], oz_s.at[which, k - 1], oz_r.at[which, k - 1], {"frame": to})

    def oz_arrival(which, k):
        z = (block_z, grad_z)[which]
        came = (frame - k + frames) % frames
        return remote(z.at[came], z.at[came], oz_s.at[which, k - 1], oz_r.at[which, k - 1], {"frame": came})

    def oz_local(which):
        own, z = ((block_own, block_z), (grad_own, grad_z))[which]
        return pltpu.make_async_copy(own.at[frame], z.at[frame], oz_l.at[which])

    def ox_copy(which, k):
        slab, out = ((block_slab, out_block), (grad_slab, out_grad))[which]
        to = (space + k) % n
        return remote(
            slab.at[to], out.at[pl.ds(cs * space, cs)], ox_s.at[which, k - 1], ox_r.at[which, k - 1], {"space": to}
        )

    def ox_arrival(which, k):
        out = (out_block, out_grad)[which]
        came = (space - k + n) % n
        piece = out.at[pl.ds(cs * came, cs)]
        return remote(piece, piece, ox_s.at[which, k - 1], ox_r.at[which, k - 1], {"space": came})

    def ox_local(which):
        slab, out = ((block_slab, out_block), (grad_slab, out_grad))[which]
        return pltpu.make_async_copy(slab.at[space], out.at[pl.ds(cs * space, cs)], ox_l.at[which])

    def send_frames(which):
        for k in range(1, frames):
            oz_copy(which, k).start()
        oz_local(which).start()

    def send_tiles(which):
        z, slab = ((block_z, block_slab), (grad_z, grad_slab))[which]
        for k in range(1, frames):
            oz_arrival(which, k).wait_recv()
        oz_local(which).wait()

        @pl.loop(0, frames)
        def _(f):
            for c in range(cf):
                rows = dot_plain(place, z[f, c])
                for t in range(n):
                    slab[t, f * cf + c] = rows[t * SLOT_PAD : (t + 1) * SLOT_PAD].astype(LOW)

        for k in range(1, n):
            ox_copy(which, k).start()
        ox_local(which).start()

    place = selection((n * SLOT_PAD, ROW_PAD), 0)
    send_frames(0)
    gres[...] = flat(cot_all, 0, wide).astype(WIDE)

    @pl.loop(0, 3)
    def _(i):
        gres[...] += dot_back(flat(ks.at[i], 0, wide), weight(first_attn + i))

    glow_pad[:, pl.ds(0, frames)] = gres[...].astype(LOW).reshape(resid.shape)
    send_tiles(0)
    gact = None
    for k in range(wt_in.shape[0]):
        term = dot_back(glow_pad[:, pl.ds(k, frames)].reshape(wide * full, channels), weight(first_temporal + k))
        gact = term if gact is None else gact + term
    pre_all = pre[...]
    sig = jax.nn.sigmoid(pre_all)
    pre[...] = gact * sig * (1.0 + pre_all * (1.0 - sig))

    @pl.loop(0, wide)
    def _(col):
        inside = (first_column + col >= 0) & (first_column + col < cs * n)
        limit = jnp.where(inside, bound, 0)
        row = lax.broadcasted_iota(jnp.int32, (full, channels), 0) % ROW_PAD
        p = jnp.where(row < limit, pre[pl.ds(col * full, full)], 0.0)
        shifted[0, col] = pltpu.roll(p, 1, 0).astype(LOW)
        shifted[1, col] = p.astype(LOW)
        shifted[2, col] = pltpu.roll(p, full - 1, 0).astype(LOW)

    ghid[...] = jnp.zeros_like(ghid)

    @pl.loop(0, taps_total)
    def _(m):
        lhs = shifted[2 - m // 3, pl.ds(2 - m % 3, cf)].reshape(cf * full, channels)
        ghid[...] += dot_back(lhs, weight(m))

    for c in range(cf):
        x = clip_all[c + 2].reshape(full, channels).astype(WIDE)
        inverse = lax.rsqrt(jnp.mean(x * x, -1, keepdims=True) + NORM_EPSILON)
        normed = x * inverse
        gn = ghid[c * full : (c + 1) * full] * gain[...]
        back = inverse * (gn - normed * jnp.mean(gn * normed, -1, keepdims=True))
        result = gres[(c + 1) * full : (c + 2) * full] + back
        grad_own[:, c] = result.astype(LOW).reshape(frames, ROW_PAD, channels)

    send_frames(1)
    send_tiles(1)
    for which in range(2):
        for k in range(1, n):
            ox_arrival(which, k).wait_recv()
        ox_local(which).wait()
        for k in range(1, n):
            p1_copy(which, k).wait_send()
            ox_copy(which, k).wait_send()
        for k in range(1, frames):
            p2_copy(which, k).wait_send()
            oz_copy(which, k).wait_send()
    for m in range(total):
        x_copy(m).wait_send()
        c0_copy(m).wait_send()
        if m < taps_total:
            y_copy(m).wait_send()
            c1_copy(m).wait_send()
            c2_copy(m).wait_send()
        else:
            for copy in quad_sends(m):
                copy.wait_send()


def per_device_strips(clip, cotangent, tile_rows, frame_start, norm_gain, w_spatial, w_temporal, w_attn):
    slots = clip.shape[1]
    breadth = clip.shape[2]
    channels = clip.shape[3]
    n = lax.axis_size("space")
    frames = lax.axis_size("frame")
    cs = breadth // n
    cf = cs // frames
    wide = cf + 2
    full = ROW_PAD * frames
    depth = w_spatial.shape[1]
    taps_total = w_spatial.shape[0]
    total = taps_total + w_temporal.shape[0] + w_attn.shape[0]
    def by_column(values, halo):
        turned = jnp.transpose(values[0], (1, 0, 2))
        return jnp.pad(turned, ((halo, halo), (0, SLOT_PAD - slots), (0, 0)))

    vmem = pl.BlockSpec(memory_space=pltpu.VMEM)
    smem = pl.BlockSpec(memory_space=pltpu.SMEM)
    hbm = pl.BlockSpec(memory_space=pl.ANY)
    dma = pltpu.SemaphoreType.DMA
    shape4 = (frames, ROW_PAD, channels)
    scratch = [
        pltpu.VMEM((total, n, depth, channels), LOW),
        pltpu.VMEM((cs + 4, n, SLOT_PAD, channels), LOW),
        pltpu.VMEM((cs + 2, n, SLOT_PAD, channels), LOW),
        pltpu.VMEM((cs + 4, ROW_PAD, channels), LOW),
        pltpu.VMEM((cs + 2, ROW_PAD, channels), LOW),
        pltpu.VMEM((wide + 2,) + shape4, LOW),
        pltpu.VMEM((wide,) + shape4, LOW),
        pltpu.VMEM((3, wide + 2, full, channels), LOW),
        pltpu.VMEM((wide * full, channels), WIDE),
        pltpu.VMEM((wide, frames + 2, ROW_PAD, channels), LOW),
        pltpu.VMEM((wide,) + shape4, LOW),
        pltpu.VMEM((3, wide) + shape4, LOW),
        pltpu.VMEM((3, wide) + shape4, LOW),
        pltpu.VMEM((wide,) + shape4, LOW),
        pltpu.VMEM((wide,) + shape4, LOW),
        pltpu.VMEM((wide * full, channels), WIDE),
        pltpu.VMEM((wide, frames + 2, ROW_PAD, channels), LOW),
        pltpu.VMEM((cf * full, channels), WIDE),
        pltpu.VMEM((frames, cf, ROW_PAD, channels), LOW),
        pltpu.VMEM((frames, cf, ROW_PAD, channels), LOW),
        pltpu.VMEM((frames, cf, ROW_PAD, channels), LOW),
        pltpu.VMEM((frames, cf, ROW_PAD, channels), LOW),
        pltpu.VMEM((n, cs, SLOT_PAD, channels), LOW),
        pltpu.VMEM((n, cs, SLOT_PAD, channels), LOW),
    ]
    scratch += [dma((total,)) for _ in range(21)]
    scratch += [dma((2, n - 1)), dma((2, n - 1)), dma((2,))]
    scratch += [dma((2, frames - 1)), dma((2, frames - 1)), dma((2,))] * 2
    scratch += [dma((2, n - 1)), dma((2, n - 1)), dma((2,))]
    out = jax.ShapeDtypeStruct((breadth, SLOT_PAD, channels), LOW)
    block, grad = pl.pallas_call(
        functools.partial(strip_kernel, n, frames, cs, cf, taps_total),
        out_shape=(out, out),
        in_specs=[smem] * 2 + [vmem] + [hbm] * 5,
        out_specs=(vmem, vmem),
        scratch_shapes=scratch,
        compiler_params=pltpu.CompilerParams(
            collective_id=0, has_side_effects=True, vmem_limit_bytes=48 * 1024 * 1024
        ),
    )(
        tile_rows, frame_start, norm_gain.reshape(1, channels),
        by_column(clip, 2), by_column(cotangent, 1), w_spatial, w_temporal, w_attn,
    )

    def by_slot(values):
        return jnp.transpose(values[:, :slots], (1, 0, 2))[None]

    return by_slot(block), by_slot(grad)


def strips_fit(mesh, clip, tile_rows):
    n = mesh.shape["space"]
    frames = mesh.shape["frame"]
    slots_all, breadth, channels = clip.shape[1:]
    return (
        mesh.shape["groups"] == 2
        and n == 4
        and breadth % (n * frames) == 0
        and slots_all // n <= SLOT_PAD
        and slots_all // 2 < ROW_PAD
        and channels % (128 * n) == 0
        and frames % 2 == 0
    )


def solution(mesh):
    placed = (
        P(("groups", "frame"), "space", None, None),
        P(("groups", "frame"), "space", None, None),
        P("groups"),
        P("groups", None),
        P(),
        P(None, "space", None),
        P(None, "space", None),
        P(None, "space", None),
    )

    def run(*arrays):
        fits = strips_fit(mesh, arrays[0], arrays[2])
        return jax.shard_map(
            per_device_strips if fits else per_device,
            mesh=mesh,
            in_specs=placed,
            out_specs=(
                P(("groups", "frame"), "space", None, None),
                P(("groups", "frame"), "space", None, None),
            ),
            check_vma=False,
        )(*arrays)

    return run
```

```python
import functools

import jax
import jax.numpy as jnp
from jax import lax
from jax.experimental import pallas as pl
from jax.experimental.pallas import tpu as pltpu
from jax.sharding import PartitionSpec as P

NORM_EPSILON = 1e-06


def passed_along(value, axis, steps):
    count = lax.axis_size(axis)
    first, last = (max(0, -steps), min(count, count - steps))
    return lax.ppermute(value, axis, [(source, source + steps) for source in range(first, last)])


def tile_rim(edge_row, offset):
    return passed_along(edge_row, "space", offset)


def frame_rim(values, offset):
    return passed_along(values, "frame", offset)


def with_faces(values, row_count):
    height = values.shape[0]
    lowest = lax.dynamic_index_in_dim(values, row_count - 1, 0, keepdims=False)
    upper_face = tile_rim(lowest, 1)
    lower_face = tile_rim(values[0], -1)
    extended = jnp.concatenate([upper_face[None], values, jnp.zeros_like(values[:1])], 0)
    position = lax.broadcasted_iota(jnp.int32, (height + 2, 1, 1), 0)
    extended = jnp.where(position == row_count + 1, lower_face[None], extended)
    return jnp.pad(extended, ((0, 0), (1, 1), (0, 0)))


def spatial_conv(extended, kernel, flipped):
    height = extended.shape[0] - 2
    breadth = extended.shape[1] - 2
    summed = None
    for tap_row in range(3):
        for tap_col in range(3):
            patches = extended[tap_row : tap_row + height, tap_col : tap_col + breadth]
            if flipped:
                product = jnp.einsum(
                    "hwd,ed->hwe",
                    patches,
                    kernel[(2 - tap_row) * 3 + 2 - tap_col],
                    preferred_element_type=jnp.float32,
                )
            else:
                product = jnp.einsum(
                    "hwd,de->hwe",
                    patches,
                    kernel[tap_row * 3 + tap_col],
                    preferred_element_type=jnp.float32,
                )
            summed = product if summed is None else summed + product
    return summed


def project(values, matrix):
    return jnp.einsum("hwd,de->hwe", values, matrix, preferred_element_type=jnp.float32)


def project_back(values, matrix):
    return jnp.einsum("hwe,de->hwd", values, matrix, preferred_element_type=jnp.float32)


def per_device(clip, cotangent, tile_rows, frame_start, norm_gain, w_spatial, w_temporal, w_attn):
    height = clip.shape[1]
    breadth = clip.shape[2]
    channels = clip.shape[3]
    frames = lax.axis_size("frame")
    frame_now = lax.axis_index("frame")
    row_count = tile_rows[lax.axis_index("space")]
    live = (lax.broadcasted_iota(jnp.int32, (height, 1, 1), 0) < row_count).astype(jnp.float32)
    score_scale = channels ** (-0.5)
    kernel, temporal, attention = (
        lax.all_gather(w_spatial, "space", axis=1, tiled=True),
        lax.all_gather(w_temporal, "space", axis=1, tiled=True),
        lax.all_gather(w_attn, "space", axis=1, tiled=True),
    )
    inputs = clip[0].astype(jnp.float32)
    inverse = lax.rsqrt(jnp.mean(inputs * inputs, -1, keepdims=True) + NORM_EPSILON)
    normed = inputs * inverse
    hidden = (normed * norm_gain * live).astype(jnp.bfloat16)
    preact = spatial_conv(with_faces(hidden, row_count), kernel, False) * live
    activated = jax.nn.silu(preact).astype(jnp.bfloat16)
    mixed = (
        project(activated, temporal[0])
        + project(frame_rim(activated, 1), temporal[1])
        + project(frame_rim(activated, 2), temporal[2])
    )
    residual = ((inputs + mixed) * live).astype(jnp.bfloat16)
    queries = project(residual, attention[0]).astype(jnp.bfloat16)
    keys_own = project(residual, attention[1]).astype(jnp.bfloat16)
    values_own = project(residual, attention[2]).astype(jnp.bfloat16)
    upstream = cotangent[0].astype(jnp.float32) * live
    grad_out = upstream.astype(jnp.bfloat16)
    grad_attended = project_back(grad_out, attention[3]).astype(jnp.bfloat16)
    pixels = height * breadth
    share = pixels // frames
    outgoing = jnp.stack(
        [
            queries.reshape(1, pixels, channels),
            keys_own.reshape(1, pixels, channels),
            values_own.reshape(1, pixels, channels),
            grad_attended.reshape(1, pixels, channels),
        ]
    )
    arrived = lax.all_to_all(outgoing, "frame", split_axis=2, concat_axis=1, tiled=True)
    query_all = arrived[0]
    key_all = arrived[1]
    value_all = arrived[2]
    upward_all = arrived[3]
    frame_ids = lax.iota(jnp.int32, frames)
    columns = (frame_now * share + lax.iota(jnp.int32, share)) % breadth
    starts = jnp.take(frame_start, columns, axis=1)
    allowed = (frame_ids[None, :, None] >= starts[:, None, :]) & (
        frame_ids[None, :, None] <= frame_ids[:, None, None]
    )
    scores = (
        jnp.einsum("fpc,gpc->fgp", query_all, key_all, preferred_element_type=jnp.float32)
        * score_scale
    )
    scores = jnp.where(allowed, scores, -jnp.inf)
    probs = jax.nn.softmax(scores, axis=1)
    probs_low = probs.astype(jnp.bfloat16)
    attended_all = jnp.einsum(
        "fgp,gpc->fpc", probs_low, value_all, preferred_element_type=jnp.float32
    ).astype(jnp.bfloat16)
    grad_probs = jnp.einsum(
        "fpc,gpc->fgp", upward_all, value_all, preferred_element_type=jnp.float32
    )
    grad_scores = probs * (grad_probs - jnp.sum(probs * grad_probs, 1, keepdims=True))
    grad_scores_low = grad_scores.astype(jnp.bfloat16)
    grad_query_all = (
        jnp.einsum("fgp,gpc->fpc", grad_scores_low, key_all, preferred_element_type=jnp.float32)
        * score_scale
    ).astype(jnp.bfloat16)
    key_terms = (
        jnp.einsum("fgp,fpc->fgpc", grad_scores_low, query_all, preferred_element_type=jnp.float32)
        * score_scale
    ).astype(jnp.bfloat16)
    grad_key_all = jnp.sum(key_terms.astype(jnp.float32), 0).astype(jnp.bfloat16)
    value_terms = jnp.einsum(
        "fgp,fpc->fgpc", probs_low, upward_all, preferred_element_type=jnp.float32
    ).astype(jnp.bfloat16)
    grad_value_all = jnp.sum(value_terms.astype(jnp.float32), 0).astype(jnp.bfloat16)
    returning = jnp.stack([attended_all, grad_query_all, grad_key_all, grad_value_all])
    came_back = lax.all_to_all(returning, "frame", split_axis=1, concat_axis=2, tiled=True)
    attended = came_back[0, 0].reshape(height, breadth, channels)
    grad_queries = came_back[1, 0].reshape(height, breadth, channels)
    grad_keys_low = came_back[2, 0].reshape(height, breadth, channels)
    grad_values_low = came_back[3, 0].reshape(height, breadth, channels)
    block_output = ((residual.astype(jnp.float32) + project(attended, attention[3])) * live).astype(
        jnp.bfloat16
    )
    grad_resid = (
        upstream
        + project_back(grad_queries, attention[0])
        + project_back(grad_keys_low, attention[1])
        + project_back(grad_values_low, attention[2])
    )
    grad_resid = grad_resid * live
    grad_low = grad_resid.astype(jnp.bfloat16)
    grad_act = (
        project_back(grad_low, temporal[0])
        + project_back(frame_rim(grad_low, -1), temporal[1])
        + project_back(frame_rim(grad_low, -2), temporal[2])
    )
    sigmoid_pre = jax.nn.sigmoid(preact)
    grad_pre = (grad_act * sigmoid_pre * (1.0 + preact * (1.0 - sigmoid_pre)) * live).astype(
        jnp.bfloat16
    )
    grad_hidden = spatial_conv(with_faces(grad_pre, row_count), kernel, True)
    grad_normed = grad_hidden * norm_gain
    grad_inputs = inverse * (
        grad_normed - normed * jnp.mean(grad_normed * normed, -1, keepdims=True)
    )
    clip_grad = ((grad_resid + grad_inputs) * live).astype(jnp.bfloat16)
    return (block_output[None], clip_grad[None])


MESH_ID = pl.DeviceIdType.MESH
LOW = jnp.bfloat16
WIDE = jnp.float32
ROW_PAD = 16
LAG = 3
SLOT_PAD = 8


def dot_plain(left, right):
    return jnp.dot(left, right, preferred_element_type=WIDE)


def dot_back(left, right):
    return lax.dot_general(left, right, (((1,), (1,)), ((), ())), preferred_element_type=WIDE)


def strip_kernel(
    n, frames, cs, cf, taps_total,
    rows_in, starts_in, gain, clip_in, cot_in, ws_in, wt_in, wa_in,
    out_block, out_grad,
    weights, clip_slab, cot_slab, clip_comp, cot_comp, clip_all, cot_all,
    shifted, pre, act_pad, resid, qs, ks, gs, att, gres, glow_pad, ghid,
    block_own, grad_own, block_z, grad_z, block_slab, grad_slab,
    x_s, x_r, c0_s, c0_r, y_s, y_r, c1_s, c1_r, c2_s, c2_r, w_loc,
    p1_s, p1_r, p1_l, p2_s, p2_r, p2_l, oz_s, oz_r, oz_l, ox_s, ox_r, ox_l,
):
    space = lax.axis_index("space")
    frame = lax.axis_index("frame")
    group = lax.axis_index("groups")
    chip = space // 2
    core = space % 2
    partner = chip * 2 + 1 - core
    across = (1 - chip) * 2 + core
    across_other = (1 - chip) * 2 + 1 - core
    wide = cf + 2
    full = ROW_PAD * frames
    depth = ws_in.shape[1]
    channels = ws_in.shape[2]
    half = depth // 2
    scale = channels ** (-0.5)

    def remote(src, dst, ssem, rsem, where):
        return pltpu.make_async_remote_copy(
            src_ref=src, dst_ref=dst, send_sem=ssem, recv_sem=rsem,
            device_id=where, device_id_type=MESH_ID,
        )

    bound = 0
    bounds = []
    for t in range(n):
        bounds.append(bound)
        bound = bound + rows_in[t]

    def selection(shape, slot_dim):
        slot = lax.broadcasted_iota(jnp.int32, shape, slot_dim)
        row = lax.broadcasted_iota(jnp.int32, shape, 1 - slot_dim)
        chosen = jnp.zeros(shape, WIDE)
        for t in range(n):
            offset = slot - t * SLOT_PAD
            hit = (offset >= 0) & (offset < rows_in[t]) & (row == offset + bounds[t])
            chosen = jnp.where(hit, 1.0, chosen)
        return chosen.astype(LOW)

    first_column = space * cs + frame * cf - 1

    barrier = pltpu.get_barrier_semaphore()
    for k in range(1, n):
        pl.semaphore_signal(barrier, inc=1, device_id={"space": (space + k) % n}, device_id_type=MESH_ID)
    for k in range(1, frames):
        pl.semaphore_signal(barrier, inc=1, device_id={"frame": (frame + k) % frames}, device_id_type=MESH_ID)
    pl.semaphore_signal(barrier, inc=1, device_id={"groups": 1 - group}, device_id_type=MESH_ID)
    pl.semaphore_wait(barrier, n + frames - 1)

    def p1_copy(which, k):
        source, slab, grow = ((clip_in, clip_slab, 4), (cot_in, cot_slab, 2))[which]
        to = (space + k) % n
        return remote(
            source.at[pl.ds(cs * to, cs + grow)], slab.at[:, space],
            p1_s.at[which, k - 1], p1_r.at[which, k - 1], {"space": to},
        )

    def p1_arrival(which, k):
        slab = (clip_slab, cot_slab)[which]
        came = (space - k + n) % n
        return remote(slab.at[:, came], slab.at[:, came], p1_s.at[which, k - 1], p1_r.at[which, k - 1], {"space": came})

    def p1_local(which):
        source, slab, grow = ((clip_in, clip_slab, 4), (cot_in, cot_slab, 2))[which]
        return pltpu.make_async_copy(source.at[pl.ds(cs * space, cs + grow)], slab.at[:, space], p1_l.at[which])

    sources = (
        [(ws_in, i) for i in range(ws_in.shape[0])]
        + [(wt_in, i) for i in range(wt_in.shape[0])]
        + [(wa_in, i) for i in range(wa_in.shape[0])]
    )
    first_temporal = ws_in.shape[0]
    first_attn = first_temporal + wt_in.shape[0]
    total = len(sources)
    my_rows = pl.ds(pl.multiple_of(group * half, half), half)
    other_rows = pl.ds(pl.multiple_of((1 - group) * half, half), half)

    def x_copy(m):
        ref, i = sources[m]
        return remote(ref.at[i, my_rows], weights.at[m, space, my_rows], x_s.at[m], x_r.at[m], {"space": across})

    def c0_copy(m):
        ref, i = sources[m]
        return remote(ref.at[i], weights.at[m, space], c0_s.at[m], c0_r.at[m], {"space": partner})

    def local_copy(m):
        ref, i = sources[m]
        return pltpu.make_async_copy(ref.at[i], weights.at[m, space], w_loc.at[m])

    for which in range(2):
        for k in range(1, n):
            p1_copy(which, k).start()
        p1_local(which).start()
    for m in range(total):
        x_copy(m).start()
        c0_copy(m).start()
        local_copy(m).start()

    def y_copy(m):
        piece = weights.at[m, across, my_rows]
        return remote(piece, piece, y_s.at[m], y_r.at[m], {"groups": 1 - group})

    def c1_copy(m):
        piece = weights.at[m, across, my_rows]
        return remote(piece, piece, c1_s.at[m], c1_r.at[m], {"space": partner})

    def c2_copy(m):
        piece = weights.at[m, across, other_rows]
        return remote(piece, piece, c2_s.at[m], c2_r.at[m], {"space": partner})

    def arrival(m, owner, rows, ssem, rsem, where):
        piece = weights.at[m, owner, rows] if rows is not None else weights.at[m, owner]
        return remote(piece, piece, ssem.at[m], rsem.at[m], where)

    def relay_first(m):
        arrival(m, across, my_rows, x_s, x_r, {"space": across}).wait_recv()
        y_copy(m).start()
        c1_copy(m).start()

    def relay_second(m):
        arrival(m, across, other_rows, y_s, y_r, {"groups": 1 - group}).wait_recv()
        c2_copy(m).start()

    def ready(m):
        arrival(m, partner, None, c0_s, c0_r, {"space": partner}).wait_recv()
        arrival(m, across_other, my_rows, c1_s, c1_r, {"space": partner}).wait_recv()
        arrival(m, across_other, other_rows, c2_s, c2_r, {"space": partner}).wait_recv()

    def compact(which):
        slab, comp = ((clip_slab, clip_comp), (cot_slab, cot_comp))[which]
        for k in range(1, n):
            p1_arrival(which, k).wait_recv()
        p1_local(which).wait()

        @pl.loop(0, slab.shape[0])
        def _(col):
            rows = jnp.concatenate([slab[col, t].astype(WIDE) for t in range(n)], 0).astype(LOW)
            comp[col] = dot_plain(pick, rows).astype(LOW)

    def p2_copy(which, k):
        comp, whole, grow = ((clip_comp, clip_all, 4), (cot_comp, cot_all, 2))[which]
        to = (frame + k) % frames
        return remote(
            comp.at[pl.ds(cf * to, cf + grow)], whole.at[:, frame],
            p2_s.at[which, k - 1], p2_r.at[which, k - 1], {"frame": to},
        )

    def p2_arrival(which, k):
        whole = (clip_all, cot_all)[which]
        came = (frame - k + frames) % frames
        return remote(whole.at[:, came], whole.at[:, came], p2_s.at[which, k - 1], p2_r.at[which, k - 1], {"frame": came})

    def p2_local(which):
        comp, whole, grow = ((clip_comp, clip_all, 4), (cot_comp, cot_all, 2))[which]
        return pltpu.make_async_copy(comp.at[pl.ds(cf * frame, cf + grow)], whole.at[:, frame], p2_l.at[which])

    pick = selection((ROW_PAD, n * SLOT_PAD), 1)
    for which in range(2):
        compact(which)
        for k in range(1, frames):
            p2_copy(which, k).start()
        p2_local(which).start()

    act_pad[:, 0:2] = jnp.zeros((wide, 2, ROW_PAD, channels), LOW)
    glow_pad[:, frames : frames + 2] = jnp.zeros((wide, 2, ROW_PAD, channels), LOW)
    ahead = total - taps_total
    behind = ahead - LAG
    for m in range(ahead):
        relay_first(m)
        if m >= LAG:
            relay_second(m - LAG)
    for k in range(1, frames):
        p2_arrival(0, k).wait_recv()
    p2_local(0).wait()

    @pl.loop(0, wide + 2)
    def _(col):
        x = clip_all[col].reshape(full, channels).astype(WIDE)
        inverse = lax.rsqrt(jnp.mean(x * x, -1, keepdims=True) + NORM_EPSILON)
        h = x * inverse * gain[...]
        shifted[0, col] = pltpu.roll(h, 1, 0).astype(LOW)
        shifted[1, col] = h.astype(LOW)
        shifted[2, col] = pltpu.roll(h, full - 1, 0).astype(LOW)

    pre[...] = jnp.zeros_like(pre)
    for m in range(total):
        local_copy(m).wait()

    def weight(m):
        return weights[m].reshape(n * depth, channels)

    @pl.loop(0, taps_total)
    def _(m):
        relay_first(m + ahead)
        relay_second(m + behind)
        ready(m)
        lhs = shifted[m // 3, pl.ds(m % 3, wide)].reshape(wide * full, channels)
        pre[...] += dot_plain(lhs, weight(m))

    for m in range(taps_total + behind, total):
        relay_second(m)

    @pl.loop(0, wide)
    def _(col):
        p = pre[pl.ds(col * full, full)]
        act_pad[col, pl.ds(2, frames)] = (p * jax.nn.sigmoid(p)).astype(LOW).reshape(frames, ROW_PAD, channels)

    for k in range(1, frames):
        p2_arrival(1, k).wait_recv()
    p2_local(1).wait()

    def flat(ref, lo, count):
        return ref[pl.ds(lo, count)].reshape(count * full, channels)

    mixed = flat(clip_all, 1, wide).astype(WIDE)
    for k in range(wt_in.shape[0]):
        ready(first_temporal + k)
        mixed += dot_plain(
            act_pad[:, pl.ds(2 - k, frames)].reshape(wide * full, channels), weight(first_temporal + k)
        )
    low = mixed.astype(LOW)
    resid[...] = low.reshape(resid.shape)

    for i in range(3):
        ready(first_attn + i)
        qs[i] = dot_plain(flat(resid, 0, wide), weight(first_attn + i)).astype(LOW).reshape(resid.shape)

    ready(first_attn + 3)
    gs[...] = dot_back(flat(cot_all, 0, wide), weight(first_attn + 3)).astype(LOW).reshape(resid.shape)

    @pl.loop(0, wide)
    def _(col):
        q = [qs[0, col, f].astype(WIDE) for f in range(frames)]
        kk = [qs[1, col, f].astype(WIDE) for f in range(frames)]
        v = [qs[2, col, f].astype(WIDE) for f in range(frames)]
        up = [gs[col, f].astype(WIDE) for f in range(frames)]
        gk = [None] * frames
        gv = [None] * frames
        column = jnp.clip(first_column + col, 0, cs * n - 1)
        for f in range(frames):
            start = starts_in[f, column]
            sc = [
                jnp.sum(q[f] * kk[g], -1, keepdims=True) * scale + jnp.where(start <= g, 0.0, -1e30)
                for g in range(f + 1)
            ]
            top = sc[0]
            for g in range(1, f + 1):
                top = jnp.maximum(top, sc[g])
            ex = [jnp.exp(s - top) for s in sc]
            den = ex[0]
            for g in range(1, f + 1):
                den = den + ex[g]
            pr = [e / den for e in ex]
            gp = [jnp.sum(up[f] * v[g], -1, keepdims=True) for g in range(f + 1)]
            dot_sum = pr[0] * gp[0]
            for g in range(1, f + 1):
                dot_sum = dot_sum + pr[g] * gp[g]
            a = None
            gq = None
            for g in range(f + 1):
                pl_low = pr[g].astype(LOW).astype(WIDE)
                sg = (pr[g] * (gp[g] - dot_sum)).astype(LOW).astype(WIDE)
                a = pl_low * v[g] if a is None else a + pl_low * v[g]
                gq = sg * kk[g] if gq is None else gq + sg * kk[g]
                tk = (sg * q[f] * scale).astype(LOW).astype(WIDE)
                tv = (pl_low * up[f]).astype(LOW).astype(WIDE)
                gk[g] = tk if gk[g] is None else gk[g] + tk
                gv[g] = tv if gv[g] is None else gv[g] + tv
            att[col, f] = a.astype(LOW)
            ks[0, col, f] = (gq * scale).astype(LOW)
        for g in range(frames):
            ks[1, col, g] = gk[g].astype(LOW)
            ks[2, col, g] = gv[g].astype(LOW)

    def spread(own, values):
        for c in range(cf):
            own[:, c] = values[c * full : (c + 1) * full].astype(LOW).reshape(frames, ROW_PAD, channels)

    block = flat(resid, 1, cf).astype(WIDE) + dot_plain(flat(att, 1, cf), weight(first_attn + 3))
    spread(block_own, block)

    def oz_copy(which, k):
        own, z = ((block_own, block_z), (grad_own, grad_z))[which]
        to = (frame + k) % frames
        return remote(own.at[to], z.at[frame], oz_s.at[which, k - 1], oz_r.at[which, k - 1], {"frame": to})

    def oz_arrival(which, k):
        z = (block_z, grad_z)[which]
        came = (frame - k + frames) % frames
        return remote(z.at[came], z.at[came], oz_s.at[which, k - 1], oz_r.at[which, k - 1], {"frame": came})

    def oz_local(which):
        own, z = ((block_own, block_z), (grad_own, grad_z))[which]
        return pltpu.make_async_copy(own.at[frame], z.at[frame], oz_l.at[which])

    def ox_copy(which, k):
        slab, out = ((block_slab, out_block), (grad_slab, out_grad))[which]
        to = (space + k) % n
        return remote(
            slab.at[to], out.at[pl.ds(cs * space, cs)], ox_s.at[which, k - 1], ox_r.at[which, k - 1], {"space": to}
        )

    def ox_arrival(which, k):
        out = (out_block, out_grad)[which]
        came = (space - k + n) % n
        piece = out.at[pl.ds(cs * came, cs)]
        return remote(piece, piece, ox_s.at[which, k - 1], ox_r.at[which, k - 1], {"space": came})

    def ox_local(which):
        slab, out = ((block_slab, out_block), (grad_slab, out_grad))[which]
        return pltpu.make_async_copy(slab.at[space], out.at[pl.ds(cs * space, cs)], ox_l.at[which])

    def send_frames(which):
        for k in range(1, frames):
            oz_copy(which, k).start()
        oz_local(which).start()

    def send_tiles(which):
        z, slab = ((block_z, block_slab), (grad_z, grad_slab))[which]
        for k in range(1, frames):
            oz_arrival(which, k).wait_recv()
        oz_local(which).wait()

        @pl.loop(0, frames)
        def _(f):
            for c in range(cf):
                rows = dot_plain(place, z[f, c])
                for t in range(n):
                    slab[t, f * cf + c] = rows[t * SLOT_PAD : (t + 1) * SLOT_PAD].astype(LOW)

        for k in range(1, n):
            ox_copy(which, k).start()
        ox_local(which).start()

    place = selection((n * SLOT_PAD, ROW_PAD), 0)
    send_frames(0)
    gres[...] = flat(cot_all, 0, wide).astype(WIDE)

    @pl.loop(0, 3)
    def _(i):
        gres[...] += dot_back(flat(ks.at[i], 0, wide), weight(first_attn + i))

    glow_pad[:, pl.ds(0, frames)] = gres[...].astype(LOW).reshape(resid.shape)
    send_tiles(0)
    gact = None
    for k in range(wt_in.shape[0]):
        term = dot_back(glow_pad[:, pl.ds(k, frames)].reshape(wide * full, channels), weight(first_temporal + k))
        gact = term if gact is None else gact + term
    pre_all = pre[...]
    sig = jax.nn.sigmoid(pre_all)
    pre[...] = gact * sig * (1.0 + pre_all * (1.0 - sig))

    @pl.loop(0, wide)
    def _(col):
        inside = (first_column + col >= 0) & (first_column + col < cs * n)
        limit = jnp.where(inside, bound, 0)
        row = lax.broadcasted_iota(jnp.int32, (full, channels), 0) % ROW_PAD
        p = jnp.where(row < limit, pre[pl.ds(col * full, full)], 0.0)
        shifted[0, col] = pltpu.roll(p, 1, 0).astype(LOW)
        shifted[1, col] = p.astype(LOW)
        shifted[2, col] = pltpu.roll(p, full - 1, 0).astype(LOW)

    ghid[...] = jnp.zeros_like(ghid)

    @pl.loop(0, taps_total)
    def _(m):
        lhs = shifted[2 - m // 3, pl.ds(2 - m % 3, cf)].reshape(cf * full, channels)
        ghid[...] += dot_back(lhs, weight(m))

    for c in range(cf):
        x = clip_all[c + 2].reshape(full, channels).astype(WIDE)
        inverse = lax.rsqrt(jnp.mean(x * x, -1, keepdims=True) + NORM_EPSILON)
        normed = x * inverse
        gn = ghid[c * full : (c + 1) * full] * gain[...]
        back = inverse * (gn - normed * jnp.mean(gn * normed, -1, keepdims=True))
        result = gres[(c + 1) * full : (c + 2) * full] + back
        grad_own[:, c] = result.astype(LOW).reshape(frames, ROW_PAD, channels)

    send_frames(1)
    send_tiles(1)
    for which in range(2):
        for k in range(1, n):
            ox_arrival(which, k).wait_recv()
        ox_local(which).wait()
        for k in range(1, n):
            p1_copy(which, k).wait_send()
            ox_copy(which, k).wait_send()
        for k in range(1, frames):
            p2_copy(which, k).wait_send()
            oz_copy(which, k).wait_send()
    for m in range(total):
        x_copy(m).wait_send()
        c0_copy(m).wait_send()
        y_copy(m).wait_send()
        c1_copy(m).wait_send()
        c2_copy(m).wait_send()


def per_device_strips(clip, cotangent, tile_rows, frame_start, norm_gain, w_spatial, w_temporal, w_attn):
    slots = clip.shape[1]
    breadth = clip.shape[2]
    channels = clip.shape[3]
    n = lax.axis_size("space")
    frames = lax.axis_size("frame")
    cs = breadth // n
    cf = cs // frames
    wide = cf + 2
    full = ROW_PAD * frames
    depth = w_spatial.shape[1]
    taps_total = w_spatial.shape[0]
    total = taps_total + w_temporal.shape[0] + w_attn.shape[0]
    def by_column(values, halo):
        turned = jnp.transpose(values[0], (1, 0, 2))
        return jnp.pad(turned, ((halo, halo), (0, SLOT_PAD - slots), (0, 0)))

    vmem = pl.BlockSpec(memory_space=pltpu.VMEM)
    smem = pl.BlockSpec(memory_space=pltpu.SMEM)
    hbm = pl.BlockSpec(memory_space=pl.ANY)
    dma = pltpu.SemaphoreType.DMA
    shape4 = (frames, ROW_PAD, channels)
    scratch = [
        pltpu.VMEM((total, n, depth, channels), LOW),
        pltpu.VMEM((cs + 4, n, SLOT_PAD, channels), LOW),
        pltpu.VMEM((cs + 2, n, SLOT_PAD, channels), LOW),
        pltpu.VMEM((cs + 4, ROW_PAD, channels), LOW),
        pltpu.VMEM((cs + 2, ROW_PAD, channels), LOW),
        pltpu.VMEM((wide + 2,) + shape4, LOW),
        pltpu.VMEM((wide,) + shape4, LOW),
        pltpu.VMEM((3, wide + 2, full, channels), LOW),
        pltpu.VMEM((wide * full, channels), WIDE),
        pltpu.VMEM((wide, frames + 2, ROW_PAD, channels), LOW),
        pltpu.VMEM((wide,) + shape4, LOW),
        pltpu.VMEM((3, wide) + shape4, LOW),
        pltpu.VMEM((3, wide) + shape4, LOW),
        pltpu.VMEM((wide,) + shape4, LOW),
        pltpu.VMEM((wide,) + shape4, LOW),
        pltpu.VMEM((wide * full, channels), WIDE),
        pltpu.VMEM((wide, frames + 2, ROW_PAD, channels), LOW),
        pltpu.VMEM((cf * full, channels), WIDE),
        pltpu.VMEM((frames, cf, ROW_PAD, channels), LOW),
        pltpu.VMEM((frames, cf, ROW_PAD, channels), LOW),
        pltpu.VMEM((frames, cf, ROW_PAD, channels), LOW),
        pltpu.VMEM((frames, cf, ROW_PAD, channels), LOW),
        pltpu.VMEM((n, cs, SLOT_PAD, channels), LOW),
        pltpu.VMEM((n, cs, SLOT_PAD, channels), LOW),
    ]
    scratch += [dma((total,)) for _ in range(11)]
    scratch += [dma((2, n - 1)), dma((2, n - 1)), dma((2,))]
    scratch += [dma((2, frames - 1)), dma((2, frames - 1)), dma((2,))] * 2
    scratch += [dma((2, n - 1)), dma((2, n - 1)), dma((2,))]
    out = jax.ShapeDtypeStruct((breadth, SLOT_PAD, channels), LOW)
    block, grad = pl.pallas_call(
        functools.partial(strip_kernel, n, frames, cs, cf, taps_total),
        out_shape=(out, out),
        in_specs=[smem] * 2 + [vmem] + [hbm] * 5,
        out_specs=(vmem, vmem),
        scratch_shapes=scratch,
        compiler_params=pltpu.CompilerParams(
            collective_id=0, has_side_effects=True, vmem_limit_bytes=48 * 1024 * 1024
        ),
    )(
        tile_rows, frame_start, norm_gain.reshape(1, channels),
        by_column(clip, 2), by_column(cotangent, 1), w_spatial, w_temporal, w_attn,
    )

    def by_slot(values):
        return jnp.transpose(values[:, :slots], (1, 0, 2))[None]

    return by_slot(block), by_slot(grad)


def strips_fit(mesh, clip, tile_rows):
    n = mesh.shape["space"]
    frames = mesh.shape["frame"]
    slots_all, breadth, channels = clip.shape[1:]
    return (
        mesh.shape["groups"] == 2
        and n == 4
        and breadth % (n * frames) == 0
        and slots_all // n <= SLOT_PAD
        and slots_all // 2 < ROW_PAD
        and channels % (128 * n) == 0
    )


def solution(mesh):
    placed = (
        P(("groups", "frame"), "space", None, None),
        P(("groups", "frame"), "space", None, None),
        P("groups"),
        P("groups", None),
        P(),
        P(None, "space", None),
        P(None, "space", None),
        P(None, "space", None),
    )

    def run(*arrays):
        fits = strips_fit(mesh, arrays[0], arrays[2])
        return jax.shard_map(
            per_device_strips if fits else per_device,
            mesh=mesh,
            in_specs=placed,
            out_specs=(
                P(("groups", "frame"), "space", None, None),
                P(("groups", "frame"), "space", None, None),
            ),
            check_vma=False,
        )(*arrays)

    return run
```

```python
import functools

import jax
import jax.numpy as jnp
from jax import lax
from jax.experimental import pallas as pl
from jax.experimental.pallas import tpu as pltpu
from jax.sharding import PartitionSpec as P

NORM_EPSILON = 1e-06


def passed_along(value, axis, steps):
    count = lax.axis_size(axis)
    first, last = (max(0, -steps), min(count, count - steps))
    return lax.ppermute(value, axis, [(source, source + steps) for source in range(first, last)])


def tile_rim(edge_row, offset):
    return passed_along(edge_row, "space", offset)


def frame_rim(values, offset):
    return passed_along(values, "frame", offset)


def with_faces(values, row_count):
    height = values.shape[0]
    lowest = lax.dynamic_index_in_dim(values, row_count - 1, 0, keepdims=False)
    upper_face = tile_rim(lowest, 1)
    lower_face = tile_rim(values[0], -1)
    extended = jnp.concatenate([upper_face[None], values, jnp.zeros_like(values[:1])], 0)
    position = lax.broadcasted_iota(jnp.int32, (height + 2, 1, 1), 0)
    extended = jnp.where(position == row_count + 1, lower_face[None], extended)
    return jnp.pad(extended, ((0, 0), (1, 1), (0, 0)))


def spatial_conv(extended, kernel, flipped):
    height = extended.shape[0] - 2
    breadth = extended.shape[1] - 2
    summed = None
    for tap_row in range(3):
        for tap_col in range(3):
            patches = extended[tap_row : tap_row + height, tap_col : tap_col + breadth]
            if flipped:
                product = jnp.einsum(
                    "hwd,ed->hwe",
                    patches,
                    kernel[(2 - tap_row) * 3 + 2 - tap_col],
                    preferred_element_type=jnp.float32,
                )
            else:
                product = jnp.einsum(
                    "hwd,de->hwe",
                    patches,
                    kernel[tap_row * 3 + tap_col],
                    preferred_element_type=jnp.float32,
                )
            summed = product if summed is None else summed + product
    return summed


def project(values, matrix):
    return jnp.einsum("hwd,de->hwe", values, matrix, preferred_element_type=jnp.float32)


def project_back(values, matrix):
    return jnp.einsum("hwe,de->hwd", values, matrix, preferred_element_type=jnp.float32)


def per_device(clip, cotangent, tile_rows, frame_start, norm_gain, w_spatial, w_temporal, w_attn):
    height = clip.shape[1]
    breadth = clip.shape[2]
    channels = clip.shape[3]
    frames = lax.axis_size("frame")
    frame_now = lax.axis_index("frame")
    row_count = tile_rows[lax.axis_index("space")]
    live = (lax.broadcasted_iota(jnp.int32, (height, 1, 1), 0) < row_count).astype(jnp.float32)
    score_scale = channels ** (-0.5)
    kernel, temporal, attention = (
        lax.all_gather(w_spatial, "space", axis=1, tiled=True),
        lax.all_gather(w_temporal, "space", axis=1, tiled=True),
        lax.all_gather(w_attn, "space", axis=1, tiled=True),
    )
    inputs = clip[0].astype(jnp.float32)
    inverse = lax.rsqrt(jnp.mean(inputs * inputs, -1, keepdims=True) + NORM_EPSILON)
    normed = inputs * inverse
    hidden = (normed * norm_gain * live).astype(jnp.bfloat16)
    preact = spatial_conv(with_faces(hidden, row_count), kernel, False) * live
    activated = jax.nn.silu(preact).astype(jnp.bfloat16)
    mixed = (
        project(activated, temporal[0])
        + project(frame_rim(activated, 1), temporal[1])
        + project(frame_rim(activated, 2), temporal[2])
    )
    residual = ((inputs + mixed) * live).astype(jnp.bfloat16)
    queries = project(residual, attention[0]).astype(jnp.bfloat16)
    keys_own = project(residual, attention[1]).astype(jnp.bfloat16)
    values_own = project(residual, attention[2]).astype(jnp.bfloat16)
    upstream = cotangent[0].astype(jnp.float32) * live
    grad_out = upstream.astype(jnp.bfloat16)
    grad_attended = project_back(grad_out, attention[3]).astype(jnp.bfloat16)
    pixels = height * breadth
    share = pixels // frames
    outgoing = jnp.stack(
        [
            queries.reshape(1, pixels, channels),
            keys_own.reshape(1, pixels, channels),
            values_own.reshape(1, pixels, channels),
            grad_attended.reshape(1, pixels, channels),
        ]
    )
    arrived = lax.all_to_all(outgoing, "frame", split_axis=2, concat_axis=1, tiled=True)
    query_all = arrived[0]
    key_all = arrived[1]
    value_all = arrived[2]
    upward_all = arrived[3]
    frame_ids = lax.iota(jnp.int32, frames)
    columns = (frame_now * share + lax.iota(jnp.int32, share)) % breadth
    starts = jnp.take(frame_start, columns, axis=1)
    allowed = (frame_ids[None, :, None] >= starts[:, None, :]) & (
        frame_ids[None, :, None] <= frame_ids[:, None, None]
    )
    scores = (
        jnp.einsum("fpc,gpc->fgp", query_all, key_all, preferred_element_type=jnp.float32)
        * score_scale
    )
    scores = jnp.where(allowed, scores, -jnp.inf)
    probs = jax.nn.softmax(scores, axis=1)
    probs_low = probs.astype(jnp.bfloat16)
    attended_all = jnp.einsum(
        "fgp,gpc->fpc", probs_low, value_all, preferred_element_type=jnp.float32
    ).astype(jnp.bfloat16)
    grad_probs = jnp.einsum(
        "fpc,gpc->fgp", upward_all, value_all, preferred_element_type=jnp.float32
    )
    grad_scores = probs * (grad_probs - jnp.sum(probs * grad_probs, 1, keepdims=True))
    grad_scores_low = grad_scores.astype(jnp.bfloat16)
    grad_query_all = (
        jnp.einsum("fgp,gpc->fpc", grad_scores_low, key_all, preferred_element_type=jnp.float32)
        * score_scale
    ).astype(jnp.bfloat16)
    key_terms = (
        jnp.einsum("fgp,fpc->fgpc", grad_scores_low, query_all, preferred_element_type=jnp.float32)
        * score_scale
    ).astype(jnp.bfloat16)
    grad_key_all = jnp.sum(key_terms.astype(jnp.float32), 0).astype(jnp.bfloat16)
    value_terms = jnp.einsum(
        "fgp,fpc->fgpc", probs_low, upward_all, preferred_element_type=jnp.float32
    ).astype(jnp.bfloat16)
    grad_value_all = jnp.sum(value_terms.astype(jnp.float32), 0).astype(jnp.bfloat16)
    returning = jnp.stack([attended_all, grad_query_all, grad_key_all, grad_value_all])
    came_back = lax.all_to_all(returning, "frame", split_axis=1, concat_axis=2, tiled=True)
    attended = came_back[0, 0].reshape(height, breadth, channels)
    grad_queries = came_back[1, 0].reshape(height, breadth, channels)
    grad_keys_low = came_back[2, 0].reshape(height, breadth, channels)
    grad_values_low = came_back[3, 0].reshape(height, breadth, channels)
    block_output = ((residual.astype(jnp.float32) + project(attended, attention[3])) * live).astype(
        jnp.bfloat16
    )
    grad_resid = (
        upstream
        + project_back(grad_queries, attention[0])
        + project_back(grad_keys_low, attention[1])
        + project_back(grad_values_low, attention[2])
    )
    grad_resid = grad_resid * live
    grad_low = grad_resid.astype(jnp.bfloat16)
    grad_act = (
        project_back(grad_low, temporal[0])
        + project_back(frame_rim(grad_low, -1), temporal[1])
        + project_back(frame_rim(grad_low, -2), temporal[2])
    )
    sigmoid_pre = jax.nn.sigmoid(preact)
    grad_pre = (grad_act * sigmoid_pre * (1.0 + preact * (1.0 - sigmoid_pre)) * live).astype(
        jnp.bfloat16
    )
    grad_hidden = spatial_conv(with_faces(grad_pre, row_count), kernel, True)
    grad_normed = grad_hidden * norm_gain
    grad_inputs = inverse * (
        grad_normed - normed * jnp.mean(grad_normed * normed, -1, keepdims=True)
    )
    clip_grad = ((grad_resid + grad_inputs) * live).astype(jnp.bfloat16)
    return (block_output[None], clip_grad[None])


MESH_ID = pl.DeviceIdType.MESH
LOW = jnp.bfloat16
WIDE = jnp.float32
ROW_PAD = 16
LAG = 3
SLOT_PAD = 8


def dot_plain(left, right):
    return jnp.dot(left, right, preferred_element_type=WIDE)


def dot_back(left, right):
    return lax.dot_general(left, right, (((1,), (1,)), ((), ())), preferred_element_type=WIDE)


def strip_kernel(
    n, frames, cs, cf, taps_total,
    rows_in, starts_in, gain, clip_in, cot_in, ws_in, wt_in, wa_in,
    out_block, out_grad,
    weights, clip_slab, cot_slab, clip_comp, cot_comp, clip_all, cot_all,
    shifted, pre, act_pad, resid, qs, ks, gs, att, gres, glow_pad, ghid,
    block_own, grad_own, block_z, grad_z, block_slab, grad_slab,
    x_s, x_r, c0_s, c0_r, y_s, y_r, c1_s, c1_r, c2_s, c2_r, w_loc,
    p1_s, p1_r, p1_l, p2_s, p2_r, p2_l, oz_s, oz_r, oz_l, ox_s, ox_r, ox_l,
):
    space = lax.axis_index("space")
    frame = lax.axis_index("frame")
    group = lax.axis_index("groups")
    chip = space // 2
    core = space % 2
    partner = chip * 2 + 1 - core
    across = (1 - chip) * 2 + core
    across_other = (1 - chip) * 2 + 1 - core
    wide = cf + 2
    full = ROW_PAD * frames
    depth = ws_in.shape[1]
    channels = ws_in.shape[2]
    half = depth // 2
    scale = channels ** (-0.5)

    def remote(src, dst, ssem, rsem, where):
        return pltpu.make_async_remote_copy(
            src_ref=src, dst_ref=dst, send_sem=ssem, recv_sem=rsem,
            device_id=where, device_id_type=MESH_ID,
        )

    bound = 0
    bounds = []
    for t in range(n):
        bounds.append(bound)
        bound = bound + rows_in[t]

    def selection(shape, slot_dim):
        slot = lax.broadcasted_iota(jnp.int32, shape, slot_dim)
        row = lax.broadcasted_iota(jnp.int32, shape, 1 - slot_dim)
        chosen = jnp.zeros(shape, WIDE)
        for t in range(n):
            offset = slot - t * SLOT_PAD
            hit = (offset >= 0) & (offset < rows_in[t]) & (row == offset + bounds[t])
            chosen = jnp.where(hit, 1.0, chosen)
        return chosen.astype(LOW)

    first_column = space * cs + frame * cf - 1

    barrier = pltpu.get_barrier_semaphore()
    for k in range(1, n):
        pl.semaphore_signal(barrier, inc=1, device_id={"space": (space + k) % n}, device_id_type=MESH_ID)
    for k in range(1, frames):
        pl.semaphore_signal(barrier, inc=1, device_id={"frame": (frame + k) % frames}, device_id_type=MESH_ID)
    pl.semaphore_signal(barrier, inc=1, device_id={"groups": 1 - group}, device_id_type=MESH_ID)
    pl.semaphore_wait(barrier, n + frames - 1)

    def p1_copy(which, k):
        source, slab, grow = ((clip_in, clip_slab, 4), (cot_in, cot_slab, 2))[which]
        to = (space + k) % n
        return remote(
            source.at[pl.ds(cs * to, cs + grow)], slab.at[:, space],
            p1_s.at[which, k - 1], p1_r.at[which, k - 1], {"space": to},
        )

    def p1_arrival(which, k):
        slab = (clip_slab, cot_slab)[which]
        came = (space - k + n) % n
        return remote(slab.at[:, came], slab.at[:, came], p1_s.at[which, k - 1], p1_r.at[which, k - 1], {"space": came})

    def p1_local(which):
        source, slab, grow = ((clip_in, clip_slab, 4), (cot_in, cot_slab, 2))[which]
        return pltpu.make_async_copy(source.at[pl.ds(cs * space, cs + grow)], slab.at[:, space], p1_l.at[which])

    sources = (
        [(ws_in, i) for i in range(ws_in.shape[0])]
        + [(wt_in, i) for i in range(wt_in.shape[0])]
        + [(wa_in, i) for i in range(wa_in.shape[0])]
    )
    first_temporal = ws_in.shape[0]
    first_attn = first_temporal + wt_in.shape[0]
    total = len(sources)
    my_rows = pl.ds(pl.multiple_of(group * half, half), half)
    other_rows = pl.ds(pl.multiple_of((1 - group) * half, half), half)

    def x_copy(m):
        ref, i = sources[m]
        return remote(ref.at[i, my_rows], weights.at[m, space, my_rows], x_s.at[m], x_r.at[m], {"space": across})

    def c0_copy(m):
        ref, i = sources[m]
        return remote(ref.at[i], weights.at[m, space], c0_s.at[m], c0_r.at[m], {"space": partner})

    def local_copy(m):
        ref, i = sources[m]
        return pltpu.make_async_copy(ref.at[i], weights.at[m, space], w_loc.at[m])

    for which in range(2):
        for k in range(1, n):
            p1_copy(which, k).start()
        p1_local(which).start()
    for m in range(total):
        x_copy(m).start()
        c0_copy(m).start()
        local_copy(m).start()

    def y_copy(m):
        piece = weights.at[m, across, my_rows]
        return remote(piece, piece, y_s.at[m], y_r.at[m], {"groups": 1 - group})

    def c1_copy(m):
        piece = weights.at[m, across, my_rows]
        return remote(piece, piece, c1_s.at[m], c1_r.at[m], {"space": partner})

    def c2_copy(m):
        piece = weights.at[m, across, other_rows]
        return remote(piece, piece, c2_s.at[m], c2_r.at[m], {"space": partner})

    def arrival(m, owner, rows, ssem, rsem, where):
        piece = weights.at[m, owner, rows] if rows is not None else weights.at[m, owner]
        return remote(piece, piece, ssem.at[m], rsem.at[m], where)

    def relay_first(m):
        arrival(m, across, my_rows, x_s, x_r, {"space": across}).wait_recv()
        y_copy(m).start()
        c1_copy(m).start()

    def relay_second(m):
        arrival(m, across, other_rows, y_s, y_r, {"groups": 1 - group}).wait_recv()
        c2_copy(m).start()

    def ready(m):
        arrival(m, partner, None, c0_s, c0_r, {"space": partner}).wait_recv()
        arrival(m, across_other, my_rows, c1_s, c1_r, {"space": partner}).wait_recv()
        arrival(m, across_other, other_rows, c2_s, c2_r, {"space": partner}).wait_recv()

    def compact(which):
        slab, comp = ((clip_slab, clip_comp), (cot_slab, cot_comp))[which]
        for k in range(1, n):
            p1_arrival(which, k).wait_recv()
        p1_local(which).wait()

        @pl.loop(0, slab.shape[0], unroll=True)
        def _(col):
            rows = jnp.concatenate([slab[col, t].astype(WIDE) for t in range(n)], 0).astype(LOW)
            comp[col] = dot_plain(pick, rows).astype(LOW)

    def p2_copy(which, k):
        comp, whole, grow = ((clip_comp, clip_all, 4), (cot_comp, cot_all, 2))[which]
        to = (frame + k) % frames
        return remote(
            comp.at[pl.ds(cf * to, cf + grow)], whole.at[:, frame],
            p2_s.at[which, k - 1], p2_r.at[which, k - 1], {"frame": to},
        )

    def p2_arrival(which, k):
        whole = (clip_all, cot_all)[which]
        came = (frame - k + frames) % frames
        return remote(whole.at[:, came], whole.at[:, came], p2_s.at[which, k - 1], p2_r.at[which, k - 1], {"frame": came})

    def p2_local(which):
        comp, whole, grow = ((clip_comp, clip_all, 4), (cot_comp, cot_all, 2))[which]
        return pltpu.make_async_copy(comp.at[pl.ds(cf * frame, cf + grow)], whole.at[:, frame], p2_l.at[which])

    pick = selection((ROW_PAD, n * SLOT_PAD), 1)
    for which in range(2):
        compact(which)
        for k in range(1, frames):
            p2_copy(which, k).start()
        p2_local(which).start()

    act_pad[:, 0:2] = jnp.zeros((wide, 2, ROW_PAD, channels), LOW)
    glow_pad[:, frames : frames + 2] = jnp.zeros((wide, 2, ROW_PAD, channels), LOW)
    ahead = total - taps_total
    behind = ahead - LAG
    for m in range(ahead):
        relay_first(m)
        if m >= LAG:
            relay_second(m - LAG)
    for k in range(1, frames):
        p2_arrival(0, k).wait_recv()
    p2_local(0).wait()

    @pl.loop(0, wide + 2, unroll=2)
    def _(col):
        x = clip_all[col].reshape(full, channels).astype(WIDE)
        inverse = lax.rsqrt(jnp.mean(x * x, -1, keepdims=True) + NORM_EPSILON)
        h = x * inverse * gain[...]
        shifted[0, col] = pltpu.roll(h, 1, 0).astype(LOW)
        shifted[1, col] = h.astype(LOW)
        shifted[2, col] = pltpu.roll(h, full - 1, 0).astype(LOW)

    pre[...] = jnp.zeros_like(pre)
    for m in range(total):
        local_copy(m).wait()

    def weight(m):
        return weights[m].reshape(n * depth, channels)

    @pl.loop(0, taps_total)
    def _(m):
        relay_first(m + ahead)
        relay_second(m + behind)
        ready(m)
        lhs = shifted[m // 3, pl.ds(m % 3, wide)].reshape(wide * full, channels)
        pre[...] += dot_plain(lhs, weight(m))

    for m in range(taps_total + behind, total):
        relay_second(m)

    @pl.loop(0, wide)
    def _(col):
        p = pre[pl.ds(col * full, full)]
        act_pad[col, pl.ds(2, frames)] = (p * jax.nn.sigmoid(p)).astype(LOW).reshape(frames, ROW_PAD, channels)

    for k in range(1, frames):
        p2_arrival(1, k).wait_recv()
    p2_local(1).wait()

    def flat(ref, lo, count):
        return ref[pl.ds(lo, count)].reshape(count * full, channels)

    mixed = flat(clip_all, 1, wide).astype(WIDE)
    for k in range(wt_in.shape[0]):
        ready(first_temporal + k)
        mixed += dot_plain(
            act_pad[:, pl.ds(2 - k, frames)].reshape(wide * full, channels), weight(first_temporal + k)
        )
    low = mixed.astype(LOW)
    resid[...] = low.reshape(resid.shape)

    for i in range(3):
        ready(first_attn + i)
        qs[i] = dot_plain(flat(resid, 0, wide), weight(first_attn + i)).astype(LOW).reshape(resid.shape)

    ready(first_attn + 3)
    gs[...] = dot_back(flat(cot_all, 0, wide), weight(first_attn + 3)).astype(LOW).reshape(resid.shape)

    @pl.loop(0, wide)
    def _(col):
        q = [qs[0, col, f].astype(WIDE) for f in range(frames)]
        kk = [qs[1, col, f].astype(WIDE) for f in range(frames)]
        v = [qs[2, col, f].astype(WIDE) for f in range(frames)]
        up = [gs[col, f].astype(WIDE) for f in range(frames)]
        gk = [None] * frames
        gv = [None] * frames
        column = jnp.clip(first_column + col, 0, cs * n - 1)
        for f in range(frames):
            start = starts_in[f, column]
            sc = [
                jnp.sum(q[f] * kk[g], -1, keepdims=True) * scale + jnp.where(start <= g, 0.0, -1e30)
                for g in range(f + 1)
            ]
            top = sc[0]
            for g in range(1, f + 1):
                top = jnp.maximum(top, sc[g])
            ex = [jnp.exp(s - top) for s in sc]
            den = ex[0]
            for g in range(1, f + 1):
                den = den + ex[g]
            pr = [e / den for e in ex]
            gp = [jnp.sum(up[f] * v[g], -1, keepdims=True) for g in range(f + 1)]
            dot_sum = pr[0] * gp[0]
            for g in range(1, f + 1):
                dot_sum = dot_sum + pr[g] * gp[g]
            a = None
            gq = None
            for g in range(f + 1):
                pl_low = pr[g].astype(LOW).astype(WIDE)
                sg = (pr[g] * (gp[g] - dot_sum)).astype(LOW).astype(WIDE)
                a = pl_low * v[g] if a is None else a + pl_low * v[g]
                gq = sg * kk[g] if gq is None else gq + sg * kk[g]
                tk = (sg * q[f] * scale).astype(LOW).astype(WIDE)
                tv = (pl_low * up[f]).astype(LOW).astype(WIDE)
                gk[g] = tk if gk[g] is None else gk[g] + tk
                gv[g] = tv if gv[g] is None else gv[g] + tv
            att[col, f] = a.astype(LOW)
            ks[0, col, f] = (gq * scale).astype(LOW)
        for g in range(frames):
            ks[1, col, g] = gk[g].astype(LOW)
            ks[2, col, g] = gv[g].astype(LOW)

    def spread(own, values):
        for c in range(cf):
            own[:, c] = values[c * full : (c + 1) * full].astype(LOW).reshape(frames, ROW_PAD, channels)

    block = flat(resid, 1, cf).astype(WIDE) + dot_plain(flat(att, 1, cf), weight(first_attn + 3))
    spread(block_own, block)

    def oz_copy(which, k):
        own, z = ((block_own, block_z), (grad_own, grad_z))[which]
        to = (frame + k) % frames
        return remote(own.at[to], z.at[frame], oz_s.at[which, k - 1], oz_r.at[which, k - 1], {"frame": to})

    def oz_arrival(which, k):
        z = (block_z, grad_z)[which]
        came = (frame - k + frames) % frames
        return remote(z.at[came], z.at[came], oz_s.at[which, k - 1], oz_r.at[which, k - 1], {"frame": came})

    def oz_local(which):
        own, z = ((block_own, block_z), (grad_own, grad_z))[which]
        return pltpu.make_async_copy(own.at[frame], z.at[frame], oz_l.at[which])

    def ox_copy(which, k):
        slab, out = ((block_slab, out_block), (grad_slab, out_grad))[which]
        to = (space + k) % n
        return remote(
            slab.at[to], out.at[pl.ds(cs * space, cs)], ox_s.at[which, k - 1], ox_r.at[which, k - 1], {"space": to}
        )

    def ox_arrival(which, k):
        out = (out_block, out_grad)[which]
        came = (space - k + n) % n
        piece = out.at[pl.ds(cs * came, cs)]
        return remote(piece, piece, ox_s.at[which, k - 1], ox_r.at[which, k - 1], {"space": came})

    def ox_local(which):
        slab, out = ((block_slab, out_block), (grad_slab, out_grad))[which]
        return pltpu.make_async_copy(slab.at[space], out.at[pl.ds(cs * space, cs)], ox_l.at[which])

    def send_frames(which):
        for k in range(1, frames):
            oz_copy(which, k).start()
        oz_local(which).start()

    def send_tiles(which):
        z, slab = ((block_z, block_slab), (grad_z, grad_slab))[which]
        for k in range(1, frames):
            oz_arrival(which, k).wait_recv()
        oz_local(which).wait()

        @pl.loop(0, frames, unroll=True)
        def _(f):
            for c in range(cf):
                rows = dot_plain(place, z[f, c])
                for t in range(n):
                    slab[t, f * cf + c] = rows[t * SLOT_PAD : (t + 1) * SLOT_PAD].astype(LOW)

        for k in range(1, n):
            ox_copy(which, k).start()
        ox_local(which).start()

    place = selection((n * SLOT_PAD, ROW_PAD), 0)
    send_frames(0)
    grad_sum = flat(cot_all, 0, wide).astype(WIDE)
    for i in range(3):
        grad_sum += dot_back(flat(ks.at[i], 0, wide), weight(first_attn + i))
    gres[...] = grad_sum

    glow_pad[:, pl.ds(0, frames)] = gres[...].astype(LOW).reshape(resid.shape)
    send_tiles(0)
    gact = None
    for k in range(wt_in.shape[0]):
        term = dot_back(glow_pad[:, pl.ds(k, frames)].reshape(wide * full, channels), weight(first_temporal + k))
        gact = term if gact is None else gact + term
    pre_all = pre[...]
    sig = jax.nn.sigmoid(pre_all)
    pre[...] = gact * sig * (1.0 + pre_all * (1.0 - sig))

    @pl.loop(0, wide)
    def _(col):
        inside = (first_column + col >= 0) & (first_column + col < cs * n)
        limit = jnp.where(inside, bound, 0)
        row = lax.broadcasted_iota(jnp.int32, (full, channels), 0) % ROW_PAD
        p = jnp.where(row < limit, pre[pl.ds(col * full, full)], 0.0)
        shifted[0, col] = pltpu.roll(p, 1, 0).astype(LOW)
        shifted[1, col] = p.astype(LOW)
        shifted[2, col] = pltpu.roll(p, full - 1, 0).astype(LOW)

    total_back = None
    for m in range(taps_total):
        lhs = shifted[2 - m // 3, pl.ds(2 - m % 3, cf)].reshape(cf * full, channels)
        term = dot_back(lhs, weight(m))
        total_back = term if total_back is None else total_back + term
    ghid[...] = total_back

    for c in range(cf):
        x = clip_all[c + 2].reshape(full, channels).astype(WIDE)
        inverse = lax.rsqrt(jnp.mean(x * x, -1, keepdims=True) + NORM_EPSILON)
        normed = x * inverse
        gn = ghid[c * full : (c + 1) * full] * gain[...]
        back = inverse * (gn - normed * jnp.mean(gn * normed, -1, keepdims=True))
        result = gres[(c + 1) * full : (c + 2) * full] + back
        grad_own[:, c] = result.astype(LOW).reshape(frames, ROW_PAD, channels)

    send_frames(1)
    send_tiles(1)
    for which in range(2):
        for k in range(1, n):
            ox_arrival(which, k).wait_recv()
        ox_local(which).wait()
        for k in range(1, n):
            p1_copy(which, k).wait_send()
            ox_copy(which, k).wait_send()
        for k in range(1, frames):
            p2_copy(which, k).wait_send()
            oz_copy(which, k).wait_send()
    for m in range(total):
        x_copy(m).wait_send()
        c0_copy(m).wait_send()
        y_copy(m).wait_send()
        c1_copy(m).wait_send()
        c2_copy(m).wait_send()


def per_device_strips(clip, cotangent, tile_rows, frame_start, norm_gain, w_spatial, w_temporal, w_attn):
    slots = clip.shape[1]
    breadth = clip.shape[2]
    channels = clip.shape[3]
    n = lax.axis_size("space")
    frames = lax.axis_size("frame")
    cs = breadth // n
    cf = cs // frames
    wide = cf + 2
    full = ROW_PAD * frames
    depth = w_spatial.shape[1]
    taps_total = w_spatial.shape[0]
    total = taps_total + w_temporal.shape[0] + w_attn.shape[0]
    def by_column(values, halo):
        turned = jnp.transpose(values[0], (1, 0, 2))
        return jnp.pad(turned, ((halo, halo), (0, SLOT_PAD - slots), (0, 0)))

    vmem = pl.BlockSpec(memory_space=pltpu.VMEM)
    smem = pl.BlockSpec(memory_space=pltpu.SMEM)
    hbm = pl.BlockSpec(memory_space=pl.ANY)
    dma = pltpu.SemaphoreType.DMA
    shape4 = (frames, ROW_PAD, channels)
    scratch = [
        pltpu.VMEM((total, n, depth, channels), LOW),
        pltpu.VMEM((cs + 4, n, SLOT_PAD, channels), LOW),
        pltpu.VMEM((cs + 2, n, SLOT_PAD, channels), LOW),
        pltpu.VMEM((cs + 4, ROW_PAD, channels), LOW),
        pltpu.VMEM((cs + 2, ROW_PAD, channels), LOW),
        pltpu.VMEM((wide + 2,) + shape4, LOW),
        pltpu.VMEM((wide,) + shape4, LOW),
        pltpu.VMEM((3, wide + 2, full, channels), LOW),
        pltpu.VMEM((wide * full, channels), WIDE),
        pltpu.VMEM((wide, frames + 2, ROW_PAD, channels), LOW),
        pltpu.VMEM((wide,) + shape4, LOW),
        pltpu.VMEM((3, wide) + shape4, LOW),
        pltpu.VMEM((3, wide) + shape4, LOW),
        pltpu.VMEM((wide,) + shape4, LOW),
        pltpu.VMEM((wide,) + shape4, LOW),
        pltpu.VMEM((wide * full, channels), WIDE),
        pltpu.VMEM((wide, frames + 2, ROW_PAD, channels), LOW),
        pltpu.VMEM((cf * full, channels), WIDE),
        pltpu.VMEM((frames, cf, ROW_PAD, channels), LOW),
        pltpu.VMEM((frames, cf, ROW_PAD, channels), LOW),
        pltpu.VMEM((frames, cf, ROW_PAD, channels), LOW),
        pltpu.VMEM((frames, cf, ROW_PAD, channels), LOW),
        pltpu.VMEM((n, cs, SLOT_PAD, channels), LOW),
        pltpu.VMEM((n, cs, SLOT_PAD, channels), LOW),
    ]
    scratch += [dma((total,)) for _ in range(11)]
    scratch += [dma((2, n - 1)), dma((2, n - 1)), dma((2,))]
    scratch += [dma((2, frames - 1)), dma((2, frames - 1)), dma((2,))] * 2
    scratch += [dma((2, n - 1)), dma((2, n - 1)), dma((2,))]
    out = jax.ShapeDtypeStruct((breadth, SLOT_PAD, channels), LOW)
    block, grad = pl.pallas_call(
        functools.partial(strip_kernel, n, frames, cs, cf, taps_total),
        out_shape=(out, out),
        in_specs=[smem] * 2 + [vmem] + [hbm] * 5,
        out_specs=(vmem, vmem),
        scratch_shapes=scratch,
        compiler_params=pltpu.CompilerParams(
            collective_id=0, has_side_effects=True, vmem_limit_bytes=48 * 1024 * 1024
        ),
    )(
        tile_rows, frame_start, norm_gain.reshape(1, channels),
        by_column(clip, 2), by_column(cotangent, 1), w_spatial, w_temporal, w_attn,
    )

    def by_slot(values):
        return jnp.transpose(values[:, :slots], (1, 0, 2))[None]

    return by_slot(block), by_slot(grad)


def strips_fit(mesh, clip, tile_rows):
    n = mesh.shape["space"]
    frames = mesh.shape["frame"]
    slots_all, breadth, channels = clip.shape[1:]
    return (
        mesh.shape["groups"] == 2
        and n == 4
        and breadth % (n * frames) == 0
        and slots_all // n <= SLOT_PAD
        and slots_all // 2 < ROW_PAD
        and channels % (128 * n) == 0
    )


def solution(mesh):
    placed = (
        P(("groups", "frame"), "space", None, None),
        P(("groups", "frame"), "space", None, None),
        P("groups"),
        P("groups", None),
        P(),
        P(None, "space", None),
        P(None, "space", None),
        P(None, "space", None),
    )

    def run(*arrays):
        fits = strips_fit(mesh, arrays[0], arrays[2])
        return jax.shard_map(
            per_device_strips if fits else per_device,
            mesh=mesh,
            in_specs=placed,
            out_specs=(
                P(("groups", "frame"), "space", None, None),
                P(("groups", "frame"), "space", None, None),
            ),
            check_vma=False,
        )(*arrays)

    return run
```
